256 devices in a mesh: ctx: 64 (over x, z, core), head: 4 (over y).
Axes of the slice: x: 4, y: 4, z: 8, core: 2. Of those that a mesh axis runs over, the one named last changes fastest.
Arguments:
- queries: bfloat16 [16384, 4096], P('ctx', 'head'), may hold values from -40 to 40
- key_rows: bfloat16 [16384, 4096], P('ctx', 'head'), may hold values from -6 to 6
- value_rows: bfloat16 [16384, 4096], P('ctx', 'head'), may hold values from -40 to 40
- log_decay: float32 [32, 16384], P('head', 'ctx'), may hold values from -1 to 0
- out_grad: bfloat16 [16384, 4096], P('ctx', 'head'), may hold values from -6 to 6
- norm_gain: float32 [4096], P('head'), may hold values from 0.1 to 1.9
Outputs:
- query_grad: bfloat16 [16384, 4096], P('ctx', 'head')
- key_grad: bfloat16 [16384, 4096], P('ctx', 'head')
- value_grad: bfloat16 [16384, 4096], P('ctx', 'head')
The draws below stay inside these ranges and needn't reach their ends.
All inputs are finite; a program needn't handle non-finite values.
Results may differ from the reference program's by a relative error of at most 0.0064.
Values sent between devices are 32-bit elements; how exact they have to be, the bound alone decides.
A program may use at most 128 MiB of HBM per device.

```python
import math
import jax
import jax.numpy as jnp
from jax import lax

HEAD_COUNT = 32
HEAD_DIM = 128
BLOCK = 256
TOKEN_COUNT = 16384


def draw_queries(key, part):
    first_key, second_key = jax.random.split(key)
    base_draw = jax.random.truncated_normal(first_key, -4.0, 4.0, (TOKEN_COUNT, HEAD_COUNT * HEAD_DIM), jnp.float32)
    row_scale = 10.0 ** jax.random.uniform(second_key, (TOKEN_COUNT, 1), jnp.float32)
    return (base_draw * row_scale).astype(jnp.bfloat16)


def draw_value_rows(key, part):
    first_key, second_key = jax.random.split(key)
    column = jnp.arange(HEAD_COUNT * HEAD_DIM) // HEAD_DIM
    head_share = column.astype(jnp.float32) / (HEAD_COUNT - 1)
    spread = jax.random.uniform(second_key, (HEAD_COUNT * HEAD_DIM,), jnp.float32)
    base_draw = jax.random.truncated_normal(first_key, -4.0, 4.0, (TOKEN_COUNT, HEAD_COUNT * HEAD_DIM), jnp.float32)
    exponent = 0.5 * spread + 0.5 * head_share
    return (base_draw * 10.0 ** exponent[None, :]).astype(jnp.bfloat16)


def draw_log_decay(key, part):
    key_sequence = jax.random.split(key, 6)
    fast_share = 0.3
    middle_share = 0.5
    picked = jax.random.uniform(key_sequence[0], (HEAD_COUNT, 1), jnp.float32)
    fast_rate = jnp.exp(jax.random.uniform(key_sequence[1], (HEAD_COUNT, 1), jnp.float32, math.log(1.0 / 50.0), math.log(1.0 / 30.0)))
    middle_rate = jnp.exp(jax.random.uniform(key_sequence[2], (HEAD_COUNT, 1), jnp.float32, math.log(0.025), math.log(0.25))) / BLOCK
    slow_rate = jnp.exp(jax.random.uniform(key_sequence[3], (HEAD_COUNT, 1), jnp.float32, math.log(0.3), math.log(1.2))) / TOKEN_COUNT
    rates = jnp.where(picked < fast_share, fast_rate, jnp.where(picked < middle_share, middle_rate, slow_rate))
    stable_level = -rates * jnp.ones((1, TOKEN_COUNT), jnp.float32)
    sudden_spike = jax.random.uniform(key_sequence[4], (HEAD_COUNT, TOKEN_COUNT), jnp.float32) < 2.0 / TOKEN_COUNT
    retained_part = jax.random.uniform(key_sequence[5], (HEAD_COUNT, TOKEN_COUNT), jnp.float32, 0.5, 0.8)
    return stable_level + jnp.where(sudden_spike, jnp.log(retained_part), 0.0)


def shard_levels(key, extent, shards, least, top_value):
    def one(position, shards_of):
        steps = jax.random.uniform(jax.random.fold_in(jax.random.fold_in(key, 6), position), (shards_of,), jnp.float32, least / len(shards), top_value / len(shards))
        return jnp.repeat(jnp.exp(steps), extent[position] // shards_of).reshape((-1,) + (1,) * (len(extent) - position - 1))

    gain = one(*shards[0])
    for cut in shards[1:]:
        gain = gain * one(*cut)
    return gain


def scatter_about(own_key, dims, deviation, reach, shards=(), kind=jnp.bfloat16):
    entries = deviation * jax.random.normal(own_key, dims, jnp.float32)
    if shards:
        entries = entries * shard_levels(own_key, dims, shards, -0.22, 0.18)
    return jnp.clip(entries, -reach, reach).astype(kind)


def setup_inputs(seed: int = 0) -> dict:
    seeds = jax.random.split(jax.random.key(seed), 7)
    return {
        "queries": draw_queries(jax.random.fold_in(seeds[6], 71), 0),
        "key_rows": scatter_about(seeds[1], (TOKEN_COUNT, HEAD_COUNT * HEAD_DIM), 1.0, 6.0, ((0, 64), (1, 4))),
        "value_rows": draw_value_rows(jax.random.fold_in(seeds[6], 71), 0),
        "log_decay": draw_log_decay(jax.random.fold_in(seeds[6], 71), 0),
        "out_grad": scatter_about(seeds[4], (TOKEN_COUNT, HEAD_COUNT * HEAD_DIM), 1.0, 6.0, ((0, 64), (1, 4))),
        "norm_gain": jnp.clip(1.0 + 0.18 * jax.random.normal(seeds[5], (HEAD_COUNT * HEAD_DIM,), jnp.float32), 0.1, 1.9),
    }


def block_weights(cumul):
    lower_mask = jnp.tril(jnp.ones((BLOCK, BLOCK), dtype=bool))
    log_gap = cumul[:, :, None] - cumul[:, None, :]
    return jnp.where(lower_mask, jnp.exp(jnp.where(lower_mask, log_gap, 0.0)), 0.0)

def block_forward(carry_state, inputs):
    query_blk, key_blk, value_blk, decay_blk = inputs
    cumul = jnp.cumsum(decay_blk, axis=1)
    ending = cumul[:, -1]
    weights = block_weights(cumul)
    scores = jnp.einsum('thd,shd->hts', query_blk.astype(jnp.float32), key_blk.astype(jnp.float32))
    attend = (scores * weights).astype(jnp.bfloat16)
    intra_out = jnp.einsum('hts,shd->thd', attend.astype(jnp.float32), value_blk.astype(jnp.float32))
    lower_start_bound = carry_state.astype(jnp.bfloat16)
    decay_query = jnp.exp(cumul).T[:, :, None]
    inter_out = jnp.einsum('thd,hde->the', query_blk.astype(jnp.float32), lower_start_bound.astype(jnp.float32)) * decay_query
    decay_key = jnp.exp(ending[:, None] - cumul).T[:, :, None]
    keyed_rows = (key_blk.astype(jnp.float32) * decay_key).astype(jnp.bfloat16)
    update = jnp.einsum('shd,she->hde', keyed_rows.astype(jnp.float32), value_blk.astype(jnp.float32))
    new_state = jnp.exp(ending)[:, None, None] * carry_state + update
    return (new_state, (intra_out + inter_out, carry_state))

def block_backward(carry_grad, inputs):
    query_blk, key_blk, value_blk, decay_blk, state_blk, grad_blk = inputs
    cumul = jnp.cumsum(decay_blk, axis=1)
    ending = cumul[:, -1]
    weights = block_weights(cumul)
    query_f = query_blk.astype(jnp.float32)
    key_f = key_blk.astype(jnp.float32)
    value_f = value_blk.astype(jnp.float32)
    grad_f = grad_blk.astype(jnp.float32)
    scores = jnp.einsum('thd,shd->hts', query_f, key_f)
    attend = (scores * weights).astype(jnp.bfloat16)
    back_scores = jnp.einsum('the,she->hts', grad_f, value_f)
    back_attend = (back_scores * weights).astype(jnp.bfloat16).astype(jnp.float32)
    lower_start_bound = state_blk.astype(jnp.bfloat16).astype(jnp.float32)
    end_low = carry_grad.astype(jnp.bfloat16).astype(jnp.float32)
    decay_query = jnp.exp(cumul).T[:, :, None]
    decay_key = jnp.exp(ending[:, None] - cumul).T[:, :, None]
    query_grad = jnp.einsum('hts,shd->thd', back_attend, key_f) + jnp.einsum('the,hde->thd', grad_f, lower_start_bound) * decay_query
    key_grad = jnp.einsum('hts,thd->shd', back_attend, query_f) + jnp.einsum('she,hde->shd', value_f, end_low) * decay_key
    value_grad = jnp.einsum('hts,the->she', attend.astype(jnp.float32), grad_f) + jnp.einsum('shd,hde->she', key_f, end_low) * decay_key
    query_scaled_rows = (query_f * decay_query).astype(jnp.bfloat16).astype(jnp.float32)
    new_grad = jnp.exp(ending)[:, None, None] * carry_grad + jnp.einsum('thd,the->hde', query_scaled_rows, grad_f)
    return (new_grad, (query_grad.astype(jnp.bfloat16), key_grad.astype(jnp.bfloat16), value_grad.astype(jnp.bfloat16)))

def reference(queries, key_rows, value_rows, log_decay, out_grad, norm_gain):
    total_rows = queries.shape[0]
    block_count = total_rows // BLOCK
    block_shape = (block_count, BLOCK, HEAD_COUNT, HEAD_DIM)
    query_blocks = queries.reshape(block_shape)
    key_blocks = key_rows.reshape(block_shape)
    value_blocks = value_rows.reshape(block_shape)
    decay_blocks = log_decay.reshape(HEAD_COUNT, block_count, BLOCK).transpose(1, 0, 2)
    zero_state = jnp.zeros((HEAD_COUNT, HEAD_DIM, HEAD_DIM), jnp.float32)
    final_state, (mixed_blocks, start_states) = lax.scan(block_forward, zero_state, (query_blocks, key_blocks, value_blocks, decay_blocks))
    mixed_out = mixed_blocks.reshape(total_rows, HEAD_COUNT, HEAD_DIM)
    feature_count = HEAD_COUNT * HEAD_DIM
    inverse = lax.rsqrt(lax.optimization_barrier(jnp.sum(mixed_out * mixed_out, axis=(1, 2))) / feature_count + 1e-06)
    scaled_grad = out_grad.reshape(total_rows, HEAD_COUNT, HEAD_DIM).astype(jnp.float32) * norm_gain.reshape(HEAD_COUNT, HEAD_DIM)
    align = lax.optimization_barrier(jnp.sum(scaled_grad * mixed_out, axis=(1, 2))) / feature_count
    grad_mixed = (inverse[:, None, None] * scaled_grad - (inverse ** 3 * align)[:, None, None] * mixed_out).astype(jnp.bfloat16)
    grad_blocks = grad_mixed.reshape(block_shape)
    first_grad, (query_grad, key_grad, value_grad) = lax.scan(block_backward, zero_state, (query_blocks, key_blocks, value_blocks, decay_blocks, start_states, grad_blocks), reverse=True)
    flat_shape = (total_rows, HEAD_COUNT * HEAD_DIM)
    return (query_grad.reshape(flat_shape), key_grad.reshape(flat_shape), value_grad.reshape(flat_shape))
```

```python
import functools

import jax
import jax.numpy as jnp
from jax import lax
from jax.experimental import pallas as pl
from jax.experimental.pallas import tpu as pltpu
from jax.sharding import PartitionSpec as P

DIM = 128
BLOCK = 256
F32 = jnp.float32
BF16 = jnp.bfloat16
HIGH = lax.Precision.HIGHEST
NN = (((1,), (0,)), ((), ()))
NT = (((1,), (1,)), ((), ()))
TN = (((0,), (0,)), ((), ()))


def dot(a, b, dims, precision=None):
    return lax.dot_general(a, b, dims, precision=precision, preferred_element_type=F32)


def ring_order(count):
    return sorted(range(count), key=lambda step: (-min(step, count - step), step))


def kernel(
    heads, nx, nz, ny,
    q_ref, k_ref, v_ref, ld_ref, og_ref, gain_ref,
    dq_ref, dk_ref, dv_ref,
    col_ref, cum_ref, end_ref, pend_ref, lrep_ref, lin_ref,
    weight_ref, attend_ref, mixed_ref, grad_ref, squery_ref, dkp_ref, dvp_ref,
    red_ref, yin_ref,
    sum_ref, srecv_ref, schip_ref, sin_ref, pout_ref, pin_ref, give_ref, erecv_ref, low_ref,
    ls_sem, lr_sem, ys_sem, yr_sem,
    cs_sem, cr_sem, us_sem, ur_sem, ds_sem, dr_sem, es_sem, er_sem,
):
    chips = nx * nz
    own_count = heads // 2
    rows = DIM // nz
    ctx = lax.axis_index("ctx")
    yy = lax.axis_index("head")
    core = lax.rem(ctx, 2)
    chip = lax.div(ctx, 2)
    mx = lax.div(chip, nz)
    mz = lax.rem(chip, nz)
    own = own_count * core
    other = own_count * (1 - core)
    partner = {"ctx": 2 * chip + (1 - core)}
    offsets = [(ox, oz) for ox in ring_order(nx) for oz in ring_order(nz)]

    def peer(ox, oz):
        px = lax.rem(mx + ox, nx)
        pz = lax.rem(mz + oz, nz)
        return px, pz, px * nz + pz

    def chip_id(index):
        return {"ctx": 2 * index + core}

    def remote(src, dst, send, recv, device):
        return pltpu.make_async_remote_copy(
            src_ref=src, dst_ref=dst, send_sem=send, recv_sem=recv,
            device_id=device, device_id_type=pl.DeviceIdType.MESH,
        )

    barrier = pltpu.get_barrier_semaphore()

    def greet(device):
        pl.semaphore_signal(
            barrier, inc=1, device_id=device, device_id_type=pl.DeviceIdType.MESH
        )

    for ox, oz in offsets:
        if (ox, oz) != (0, 0):
            greet(chip_id(peer(ox, oz)[2]))
    greet(partner)
    for oy in range(1, ny):
        greet({"head": lax.rem(yy + oy, ny)})

    def head_cols(h):
        return pl.ds(pl.multiple_of(h * DIM, DIM), DIM)

    step_u = lax.broadcasted_iota(jnp.int32, (BLOCK, BLOCK), 0)
    step_t = lax.broadcasted_iota(jnp.int32, (BLOCK, BLOCK), 1)
    cum = dot(ld_ref[...], (step_u <= step_t).astype(F32), NN, HIGH)
    cum_ref[...] = cum
    pick = lax.broadcasted_iota(jnp.int32, (heads, DIM), 0)
    for h in range(heads):
        col = dot(cum, (pick == h).astype(F32), TN, HIGH)
        col_ref[h] = col
        end_ref[h] = col[BLOCK - 1 : BLOCK, :]

    def decay_key(h):
        return jnp.exp(end_ref[h] - col_ref[h])

    def decay_query(h):
        return jnp.exp(col_ref[h])

    def key_sum(i, base):
        h = base + i
        keyed = (k_ref[:, head_cols(h)].astype(F32) * decay_key(h)).astype(BF16)
        sum_ref[0, h] = dot(keyed, v_ref[:, head_cols(h)], TN)
        return base

    def core_copy(way, i):
        return remote(
            sum_ref.at[way, other + i], srecv_ref.at[way, i],
            cs_sem.at[way, i], cr_sem.at[way, i], partner,
        )

    def log_copy(slot):
        return remote(end_ref, pend_ref, ls_sem.at[slot], lr_sem.at[slot], partner)

    lax.fori_loop(0, own_count, key_sum, other)
    lax.fori_loop(0, own_count, key_sum, own)

    pl.semaphore_wait(barrier, chips - 1 + 1 + ny - 1)

    log_copy(chips).start()
    for i in range(own_count):
        core_copy(0, i).start()

    log_copy(chips).wait_recv()
    for i in range(own_count):
        lrep_ref[i] = end_ref[own + i] + pend_ref[own + i]

    def rate_copy(ox, oz):
        px, pz, index = peer(ox, oz)
        return remote(
            lrep_ref.at[px], lin_ref.at[chip], ls_sem.at[index], lr_sem.at[chip], chip_id(index)
        )

    for ox, oz in offsets:
        if (ox, oz) != (0, 0):
            rate_copy(ox, oz).start()
    lin_ref[chip] = lrep_ref[mx]

    def up_copy(way, ox, oz):
        px, pz, index = peer(ox, oz)
        return remote(
            schip_ref.at[way, px, pl.ds(pl.multiple_of(pz * rows, rows), rows)],
            sin_ref.at[way, chip],
            us_sem.at[way, index], ur_sem.at[way, chip], chip_id(index),
        )

    def up_arrival(way, index):
        return remote(
            schip_ref.at[way, 0, pl.ds(0, rows)], sin_ref.at[way, index],
            us_sem.at[way, index], ur_sem.at[way, index], chip_id(index),
        )

    def down_copy(way, ox, oz):
        px, pz, index = peer(ox, oz)
        return remote(
            pout_ref.at[way, index],
            pin_ref.at[way, mx, pl.ds(pl.multiple_of(mz * rows, rows), rows)],
            ds_sem.at[way, index], dr_sem.at[way, chip], chip_id(index),
        )

    def down_arrival(way, px, pz):
        index = px * nz + pz
        return remote(
            pout_ref.at[way, index],
            pin_ref.at[way, px, pl.ds(pl.multiple_of(pz * rows, rows), rows)],
            ds_sem.at[way, index], dr_sem.at[way, index], chip_id(index),
        )

    def give_copy(way, h):
        return remote(
            give_ref.at[way, h], erecv_ref.at[way, h],
            es_sem.at[way, h], er_sem.at[way, h], partner,
        )

    my_rows = pl.ds(pl.multiple_of(mz * rows, rows), rows)

    def send_up(way, cc):
        for i in range(own_count):
            core_copy(way, i).wait_recv()
        for ox in ring_order(nx):
            h = lax.rem(mx + ox, nx)
            one = jnp.ones((1, DIM), F32)
            mine = jnp.where(cc == 0, jnp.exp(pend_ref[own + h]), one)
            theirs = jnp.where(cc == 0, one, jnp.exp(end_ref[own + h]))
            schip_ref[way, h] = mine * sum_ref[way, own + h] + theirs * srecv_ref[way, h]
            for oz in ring_order(nz):
                if (ox, oz) != (0, 0):
                    up_copy(way, ox, oz).start()
        sin_ref[way, chip] = schip_ref[way, mx, my_rows, :]

    def scan_and_send_down(way):
        for ox, oz in offsets:
            if (ox, oz) != (0, 0):
                up_arrival(way, peer(ox, oz)[2]).wait_recv()

        def one(step, carry):
            index = step if way == 0 else chips - 1 - step
            pout_ref[way, index] = carry
            return jnp.exp(lin_ref[index]) * carry + sin_ref[way, index]

        lax.fori_loop(0, chips, one, jnp.zeros((rows, DIM), F32))
        for ox, oz in offsets:
            if (ox, oz) != (0, 0):
                down_copy(way, ox, oz).start()
        pin_ref[way, mx, my_rows, :] = pout_ref[way, chip]

    def finish_own(way, cc):
        for ox in ring_order(nx):
            h = lax.rem(mx + ox, nx)
            for oz in ring_order(nz):
                if (ox, oz) != (0, 0):
                    px, pz, _ = peer(ox, oz)
                    down_arrival(way, px, pz).wait_recv()
            one = jnp.ones((1, DIM), F32)
            none = jnp.zeros((1, DIM), F32)
            before = pin_ref[way, h]
            give_ref[way, h] = (
                jnp.where(cc == 0, jnp.exp(end_ref[own + h]), one) * before
                + jnp.where(cc == 0, one, none) * sum_ref[way, own + h]
            )
            give_copy(way, h).start()
            low_ref[way, own + h] = (
                jnp.where(cc == 0, one, jnp.exp(pend_ref[own + h])) * before
                + jnp.where(cc == 0, none, one) * srecv_ref[way, h]
            ).astype(BF16)

    def finish_other(way):
        for h in range(own_count):
            give_copy(way, h).wait_recv()
            low_ref[way, other + h] = erecv_ref[way, h].astype(BF16)

    send_up(0, core)

    lower = step_t <= step_u

    def inner_out(h, carry):
        col = col_ref[h]
        gap = jnp.concatenate([col, col], axis=1) - cum_ref[pl.ds(h, 1), :]
        weight = jnp.where(lower, jnp.exp(jnp.where(lower, gap, 0.0)), 0.0)
        weight_ref[h] = weight
        q = q_ref[:, head_cols(h)]
        attend = (dot(q, k_ref[:, head_cols(h)], NT) * weight).astype(BF16)
        attend_ref[h] = attend
        mixed_ref[h] = dot(attend, v_ref[:, head_cols(h)], NN)
        squery_ref[h] = (q.astype(F32) * decay_query(h)).astype(BF16)
        return carry

    lax.fori_loop(0, heads, inner_out, 0)

    for ox, oz in offsets:
        if (ox, oz) != (0, 0):
            index = peer(ox, oz)[2]
            remote(
                lrep_ref.at[0], lin_ref.at[index], ls_sem.at[index], lr_sem.at[index],
                chip_id(index),
            ).wait_recv()

    scan_and_send_down(0)
    finish_own(0, core)

    def scaled_grad(h):
        return og_ref[:, head_cols(h)].astype(F32) * gain_ref[pl.ds(h, 1), :]

    def outer_out(i, carry):
        base, power, align = carry
        h = base + i
        mixed = mixed_ref[h] + dot(q_ref[:, head_cols(h)], low_ref[0, h], NN) * decay_query(h)
        mixed_ref[h] = mixed
        return base, power + mixed * mixed, align + scaled_grad(h) * mixed

    zero = jnp.zeros((BLOCK, DIM), F32)
    _, power, align = lax.fori_loop(0, own_count, outer_out, (own, zero, zero))
    finish_other(0)
    _, power, align = lax.fori_loop(0, own_count, outer_out, (other, power, align))

    ones = jnp.ones((8, DIM), F32)
    sums_row = lax.broadcasted_iota(jnp.int32, (8, BLOCK), 0)
    red_ref[...] = jnp.where(
        sums_row < 4, dot(ones, power, NT, HIGH), dot(ones, align, NT, HIGH)
    )

    def sums_copy(oy):
        to = lax.rem(yy + oy, ny)
        return remote(red_ref, yin_ref.at[yy], ys_sem.at[to], yr_sem.at[yy], {"head": to})

    def sums_arrival(oy):
        source = lax.rem(yy + oy, ny)
        return remote(
            red_ref, yin_ref.at[source], ys_sem.at[source], yr_sem.at[source], {"head": source}
        )

    for oy in range(1, ny):
        sums_copy(oy).start()
    yin_ref[yy] = red_ref[...]
    for oy in range(1, ny):
        sums_arrival(oy).wait_recv()
    total = yin_ref[0]
    for index in range(1, ny):
        total = total + yin_ref[index]
    features = heads * DIM * ny
    inverse = lax.rsqrt(total[0:1, :] / features + 1e-6)
    factor = inverse * inverse * inverse * (total[4:5, :] / features)
    pair = jnp.where(sums_row < 4, inverse, factor)
    pick8 = lax.broadcasted_iota(jnp.int32, (8, DIM), 0)
    inverse_col = dot(pair, (pick8 == 0).astype(F32), TN, HIGH)
    factor_col = dot(pair, (pick8 == 4).astype(F32), TN, HIGH)

    def grad_sum(i, base):
        h = base + i
        grad = (inverse_col * scaled_grad(h) - factor_col * mixed_ref[h]).astype(BF16)
        grad_ref[h] = grad
        sum_ref[1, h] = dot(squery_ref[h], grad, TN)
        return base

    lax.fori_loop(0, own_count, grad_sum, other)
    for i in range(own_count):
        core_copy(1, i).start()
    lax.fori_loop(0, own_count, grad_sum, own)
    send_up(1, 1 - core)

    def inner_grads(h, carry):
        cols = head_cols(h)
        grad = grad_ref[h]
        back = (dot(grad, v_ref[:, cols], NT) * weight_ref[h]).astype(BF16)
        dq = dot(back, k_ref[:, cols], NN) + dot(grad, low_ref[0, h], NT) * decay_query(h)
        dq_ref[:, cols] = dq.astype(BF16)
        dkp_ref[h] = dot(back, q_ref[:, cols], TN)
        dvp_ref[h] = dot(attend_ref[h], grad, TN)
        return carry

    lax.fori_loop(0, heads, inner_grads, 0)

    scan_and_send_down(1)
    finish_own(1, 1 - core)

    def outer_grads(i, base):
        h = base + i
        cols = head_cols(h)
        decay = decay_key(h)
        low = low_ref[1, h]
        dk_ref[:, cols] = (dkp_ref[h] + dot(v_ref[:, cols], low, NT) * decay).astype(BF16)
        dv_ref[:, cols] = (dvp_ref[h] + dot(k_ref[:, cols], low, NN) * decay).astype(BF16)
        return base

    lax.fori_loop(0, own_count, outer_grads, own)
    finish_other(1)
    lax.fori_loop(0, own_count, outer_grads, other)

    log_copy(chips).wait_send()
    for oy in range(1, ny):
        sums_copy(oy).wait_send()
    for ox, oz in offsets:
        if (ox, oz) != (0, 0):
            rate_copy(ox, oz).wait_send()
    for way in range(2):
        for i in range(own_count):
            core_copy(way, i).wait_send()
            give_copy(way, i).wait_send()
        for ox, oz in offsets:
            if (ox, oz) != (0, 0):
                up_copy(way, ox, oz).wait_send()
                down_copy(way, ox, oz).wait_send()


def body(queries, key_rows, value_rows, log_decay, out_grad, norm_gain):
    length, width = queries.shape
    heads = width // DIM
    ny = lax.axis_size("head")
    chips = lax.axis_size("ctx") // 2
    nx = heads // 2
    nz = chips // nx
    half = heads // 2
    rows = DIM // nz
    out = jax.ShapeDtypeStruct((length, width), BF16)
    vmem = pl.BlockSpec(memory_space=pltpu.VMEM)
    dma = pltpu.SemaphoreType.DMA
    return pl.pallas_call(
        functools.partial(kernel, heads, nx, nz, ny),
        out_shape=(out, out, out),
        in_specs=[vmem] * 6,
        out_specs=(vmem, vmem, vmem),
        scratch_shapes=[
            pltpu.VMEM((heads, BLOCK, DIM), F32),
            pltpu.VMEM((heads, BLOCK), F32),
            pltpu.VMEM((heads, 1, DIM), F32),
            pltpu.VMEM((heads, 1, DIM), F32),
            pltpu.VMEM((half, 1, DIM), F32),
            pltpu.VMEM((chips, 1, DIM), F32),
            pltpu.VMEM((heads, BLOCK, BLOCK), F32),
            pltpu.VMEM((heads, BLOCK, BLOCK), BF16),
            pltpu.VMEM((heads, BLOCK, DIM), F32),
            pltpu.VMEM((heads, BLOCK, DIM), BF16),
            pltpu.VMEM((heads, BLOCK, DIM), BF16),
            pltpu.VMEM((heads, BLOCK, DIM), F32),
            pltpu.VMEM((heads, BLOCK, DIM), F32),
            pltpu.VMEM((8, BLOCK), F32),
            pltpu.VMEM((ny, 8, BLOCK), F32),
            pltpu.VMEM((2, heads, DIM, DIM), F32),
            pltpu.VMEM((2, half, DIM, DIM), F32),
            pltpu.VMEM((2, half, DIM, DIM), F32),
            pltpu.VMEM((2, chips, rows, DIM), F32),
            pltpu.VMEM((2, chips, rows, DIM), F32),
            pltpu.VMEM((2, half, DIM, DIM), F32),
            pltpu.VMEM((2, half, DIM, DIM), F32),
            pltpu.VMEM((2, half, DIM, DIM), F32),
            pltpu.VMEM((2, heads, DIM, DIM), BF16),
            dma((chips + 1,)),
            dma((chips + 1,)),
            dma((ny,)),
            dma((ny,)),
            dma((2, half)),
            dma((2, half)),
            dma((2, chips)),
            dma((2, chips)),
            dma((2, chips)),
            dma((2, chips)),
            dma((2, half)),
            dma((2, half)),
        ],
        compiler_params=pltpu.CompilerParams(
            collective_id=0, has_side_effects=True, vmem_limit_bytes=60 * 2**20
        ),
        name="lightning",
    )(
        queries, key_rows, value_rows, log_decay, out_grad,
        norm_gain.reshape(heads, DIM),
    )


def solution(mesh):
    return jax.shard_map(
        body,
        mesh=mesh,
        in_specs=(
            P("ctx", "head"),
            P("ctx", "head"),
            P("ctx", "head"),
            P("head", "ctx"),
            P("ctx", "head"),
            P("head"),
        ),
        out_specs=(P("ctx", "head"), P("ctx", "head"), P("ctx", "head")),
        check_vma=False,
    )
```

```python
import functools

import jax
import jax.numpy as jnp
from jax import lax
from jax.experimental import pallas as pl
from jax.experimental.pallas import tpu as pltpu
from jax.sharding import PartitionSpec as P

DIM = 128
BLOCK = 256
F32 = jnp.float32
BF16 = jnp.bfloat16
HIGH = lax.Precision.HIGHEST
NN = (((1,), (0,)), ((), ()))
NT = (((1,), (1,)), ((), ()))
TN = (((0,), (0,)), ((), ()))


def dot(a, b, dims, precision=None):
    return lax.dot_general(a, b, dims, precision=precision, preferred_element_type=F32)


def ring_order(count):
    return sorted(range(count), key=lambda step: (-min(step, count - step), step))


def split3(x, axis):
    high = x.astype(BF16)
    rest = x - high.astype(F32)
    middle = rest.astype(BF16)
    low = (rest - middle.astype(F32)).astype(BF16)
    return jnp.concatenate([high, middle, low], axis=axis)


def kernel(
    heads, nx, nz, ny,
    q_hbm, k_hbm, v_hbm, ld_hbm, og_hbm, gain_hbm,
    dq_ref, dk_ref, dv_ref,
    q_ref, k_ref, v_ref, ld_ref, og_ref, gain_ref,
    col_ref, cum_ref, end_ref, pend_ref, lrep_ref, lin_ref, rate_ref,
    weight_ref, attend_ref, mixed_ref, grad_ref, squery_ref, dkp_ref, dvp_ref,
    power_ref, align_ref, red_ref, yin_ref,
    sum_ref, srecv_ref, schip_ref, sin_ref, pout_ref, pin_ref, give_ref, erecv_ref, low_ref,
    in_sem, ls_sem, lr_sem, ys_sem, yr_sem,
    cs_sem, cr_sem, us_sem, ur_sem, ds_sem, dr_sem, es_sem, er_sem,
):
    chips = nx * nz
    own_count = heads // 2
    rows = DIM // nz
    ctx = lax.axis_index("ctx")
    yy = lax.axis_index("head")
    core = lax.rem(ctx, 2)
    chip = lax.div(ctx, 2)
    mx = lax.div(chip, nz)
    mz = lax.rem(chip, nz)
    own = own_count * core
    other = own_count * (1 - core)
    partner = {"ctx": 2 * chip + (1 - core)}
    xs = ring_order(nx)
    zs = ring_order(nz)
    px = [lax.rem(mx + o, nx) for o in range(nx)]
    pz = [lax.rem(mz + o, nz) for o in range(nz)]
    index_of = [[px[ox] * nz + pz[oz] for oz in range(nz)] for ox in range(nx)]
    offsets = [(ox, oz) for ox in xs for oz in zs if (ox, oz) != (0, 0)]
    turn = [px[ox] for ox in xs]

    def chip_id(index):
        return {"ctx": 2 * index + core}

    def remote(src, dst, send, recv, device):
        return pltpu.make_async_remote_copy(
            src_ref=src, dst_ref=dst, send_sem=send, recv_sem=recv,
            device_id=device, device_id_type=pl.DeviceIdType.MESH,
        )

    barrier = pltpu.get_barrier_semaphore()

    def greet(device):
        pl.semaphore_signal(
            barrier, inc=1, device_id=device, device_id_type=pl.DeviceIdType.MESH
        )

    for ox, oz in offsets:
        greet(chip_id(index_of[ox][oz]))
    greet(partner)
    for oy in range(1, ny):
        greet({"head": lax.rem(yy + oy, ny)})

    loads = [
        pltpu.make_async_copy(src, dst, in_sem.at[n])
        for n, (src, dst) in enumerate(
            [
                (ld_hbm, ld_ref), (k_hbm, k_ref), (v_hbm, v_ref),
                (q_hbm, q_ref), (og_hbm, og_ref), (gain_hbm, gain_ref),
            ]
        )
    ]
    for load in loads:
        load.start()

    def head_cols(h):
        return pl.ds(pl.multiple_of(h * DIM, DIM), DIM)

    step_u = lax.broadcasted_iota(jnp.int32, (BLOCK, BLOCK), 0)
    step_t = lax.broadcasted_iota(jnp.int32, (BLOCK, BLOCK), 1)
    loads[0].wait()
    cum = dot(ld_ref[...], (step_u <= step_t).astype(F32), NN, HIGH)
    cum_ref[...] = cum
    pick = lax.broadcasted_iota(jnp.int32, (heads, DIM), 0)
    for h in range(heads):
        col = dot(cum, (pick == h).astype(F32), TN, HIGH)
        col_ref[h] = col
        end_ref[h] = col[BLOCK - 1 : BLOCK, :]
    loads[1].wait()
    loads[2].wait()

    def decay_key(h):
        return jnp.exp(end_ref[h] - col_ref[h])

    def decay_query(h):
        return jnp.exp(col_ref[h])

    def key_sum(i, base):
        h = base + i
        keyed = (k_ref[:, head_cols(h)].astype(F32) * decay_key(h)).astype(BF16)
        sum_ref[0, h] = dot(keyed, v_ref[:, head_cols(h)], TN)
        return base

    def core_copy(way, i):
        return remote(
            sum_ref.at[way, other + i], srecv_ref.at[way, i],
            cs_sem.at[way, i], cr_sem.at[way, i], partner,
        )

    log_copy = remote(end_ref, pend_ref, ls_sem.at[chips], lr_sem.at[chips], partner)

    lax.fori_loop(0, own_count, key_sum, other)
    lax.fori_loop(0, own_count, key_sum, own)
    loads[3].wait()

    pl.semaphore_wait(barrier, chips - 1 + 1 + ny - 1)

    log_copy.start()
    for h in turn:
        core_copy(0, h).start()

    log_copy.wait_recv()
    for i in range(own_count):
        lrep_ref[i] = end_ref[own + i] + pend_ref[own + i]

    def rate_copy(ox, oz):
        index = index_of[ox][oz]
        return remote(
            lrep_ref.at[px[ox]], lin_ref.at[chip], ls_sem.at[index], lr_sem.at[chip],
            chip_id(index),
        )

    def rate_arrival(ox, oz):
        index = index_of[ox][oz]
        return remote(
            lrep_ref.at[0], lin_ref.at[index], ls_sem.at[index], lr_sem.at[index],
            chip_id(index),
        )

    def up_copy(way, ox, oz):
        index = index_of[ox][oz]
        return remote(
            schip_ref.at[way, px[ox], pl.ds(pl.multiple_of(pz[oz] * rows, rows), rows)],
            sin_ref.at[way, chip],
            us_sem.at[way, index], ur_sem.at[way, chip], chip_id(index),
        )

    def up_arrival(way, ox, oz):
        index = index_of[ox][oz]
        return remote(
            schip_ref.at[way, 0, pl.ds(0, rows)], sin_ref.at[way, index],
            us_sem.at[way, index], ur_sem.at[way, index], chip_id(index),
        )

    my_rows = pl.ds(pl.multiple_of(mz * rows, rows), rows)

    def down_copy(way, ox, oz):
        index = index_of[ox][oz]
        return remote(
            pout_ref.at[way, index], pin_ref.at[way, mx, my_rows],
            ds_sem.at[way, index], dr_sem.at[way, chip], chip_id(index),
        )

    def down_arrival(way, ox, oz):
        index = index_of[ox][oz]
        return remote(
            pout_ref.at[way, index],
            pin_ref.at[way, px[ox], pl.ds(pl.multiple_of(pz[oz] * rows, rows), rows)],
            ds_sem.at[way, index], dr_sem.at[way, index], chip_id(index),
        )

    def give_copy(way, h):
        return remote(
            give_ref.at[way, h], erecv_ref.at[way, h],
            es_sem.at[way, h], er_sem.at[way, h], partner,
        )

    one = jnp.ones((1, DIM), F32)
    none = jnp.zeros((1, DIM), F32)

    def send_up(way, cc, n):
        ox, h = xs[n], turn[n]
        core_copy(way, h).wait_recv()
        mine = jnp.where(cc == 0, jnp.exp(pend_ref[own + h]), one)
        theirs = jnp.where(cc == 0, one, jnp.exp(end_ref[own + h]))
        schip_ref[way, h] = mine * sum_ref[way, own + h] + theirs * srecv_ref[way, h]
        for oz in zs:
            if (ox, oz) != (0, 0):
                up_copy(way, ox, oz).start()
            else:
                sin_ref[way, chip] = schip_ref[way, mx, my_rows, :]

    def scan_and_send_down(way):
        for ox, oz in offsets:
            up_arrival(way, ox, oz).wait_recv()

        def advance(step, carry):
            index = step if way == 0 else chips - 1 - step
            pout_ref[way, index] = carry
            return rate_ref[index] * carry + sin_ref[way, index]

        lax.fori_loop(0, chips, advance, jnp.zeros((rows, DIM), F32), unroll=8)
        for ox, oz in offsets:
            down_copy(way, ox, oz).start()
        pin_ref[way, mx, my_rows, :] = pout_ref[way, chip]

    def take_own(way, cc, n):
        ox, h = xs[n], turn[n]
        for oz in zs:
            if (ox, oz) != (0, 0):
                down_arrival(way, ox, oz).wait_recv()
        before = pin_ref[way, h]
        give_ref[way, h] = (
            jnp.where(cc == 0, jnp.exp(end_ref[own + h]), one) * before
            + jnp.where(cc == 0, one, none) * sum_ref[way, own + h]
        )
        give_copy(way, h).start()
        low_ref[way, own + h] = (
            jnp.where(cc == 0, one, jnp.exp(pend_ref[own + h])) * before
            + jnp.where(cc == 0, none, one) * srecv_ref[way, h]
        ).astype(BF16)

    def take_other(way, n):
        h = turn[n]
        give_copy(way, h).wait_recv()
        low_ref[way, other + h] = erecv_ref[way, h].astype(BF16)

    def deliver(way, cc, use):
        for n in range(own_count):
            take_own(way, cc, n)
            if n > 1:
                take_other(way, n - 2)
                use(other + turn[n - 2])
            use(own + turn[n])
        for n in range(own_count - 2, own_count):
            take_other(way, n)
            use(other + turn[n])

    for ox, oz in offsets:
        rate_copy(ox, oz).start()
    lin_ref[chip] = lrep_ref[mx]
    for n in range(own_count):
        send_up(0, core, n)

    lower = step_t <= step_u

    def inner_out(h, carry):
        col = col_ref[h]
        gap = jnp.concatenate([col, col], axis=1) - cum_ref[pl.ds(h, 1), :]
        weight = jnp.where(lower, jnp.exp(jnp.where(lower, gap, 0.0)), 0.0)
        weight_ref[h] = weight
        q = q_ref[:, head_cols(h)]
        attend = (dot(q, k_ref[:, head_cols(h)], NT) * weight).astype(BF16)
        attend_ref[h] = attend
        mixed_ref[h] = dot(attend, v_ref[:, head_cols(h)], NN)
        squery_ref[h] = (q.astype(F32) * decay_query(h)).astype(BF16)
        return carry

    lax.fori_loop(0, heads, inner_out, 0)
    loads[4].wait()
    loads[5].wait()
    power_ref[...] = jnp.zeros_like(power_ref)
    align_ref[...] = jnp.zeros_like(align_ref)

    for ox, oz in offsets:
        rate_arrival(ox, oz).wait_recv()
    rate_ref[...] = jnp.exp(lin_ref[...])

    scan_and_send_down(0)

    def scaled_grad(h):
        return og_ref[:, head_cols(h)].astype(F32) * gain_ref[pl.ds(h, 1), :]

    def outer_out(h):
        mixed = mixed_ref[h] + dot(q_ref[:, head_cols(h)], low_ref[0, h], NN) * decay_query(h)
        mixed_ref[h] = mixed
        power_ref[...] += mixed * mixed
        align_ref[...] += scaled_grad(h) * mixed

    deliver(0, core, outer_out)

    ones = jnp.ones((8, 3 * DIM), BF16)
    sums_row = lax.broadcasted_iota(jnp.int32, (8, BLOCK), 0)
    red_ref[...] = jnp.where(
        sums_row < 4,
        dot(ones, split3(power_ref[...], 1), NT),
        dot(ones, split3(align_ref[...], 1), NT),
    )

    def sums_copy(oy):
        to = lax.rem(yy + oy, ny)
        return remote(red_ref, yin_ref.at[yy], ys_sem.at[to], yr_sem.at[yy], {"head": to})

    def sums_arrival(oy):
        source = lax.rem(yy + oy, ny)
        return remote(
            red_ref, yin_ref.at[source], ys_sem.at[source], yr_sem.at[source], {"head": source}
        )

    for oy in range(1, ny):
        sums_copy(oy).start()
    yin_ref[yy] = red_ref[...]
    for oy in range(1, ny):
        sums_arrival(oy).wait_recv()
    total = yin_ref[0]
    for index in range(1, ny):
        total = total + yin_ref[index]
    features = heads * DIM * ny
    inverse = lax.rsqrt(total[0:1, :] / features + 1e-6)
    factor = inverse * inverse * inverse * (total[4:5, :] / features)
    pair_row = lax.broadcasted_iota(jnp.int32, (16, BLOCK), 0)
    pair = split3(jnp.where(pair_row < 8, inverse, factor), 0)
    pick_row = lax.rem(lax.broadcasted_iota(jnp.int32, (48, DIM), 0), 16)
    inverse_col = dot(pair, jnp.where(pick_row == 0, 1.0, 0.0).astype(BF16), TN)
    factor_col = dot(pair, jnp.where(pick_row == 8, 1.0, 0.0).astype(BF16), TN)
    power_ref[...] = inverse_col
    align_ref[...] = factor_col

    def grad_sum(h):
        grad = (power_ref[...] * scaled_grad(h) - align_ref[...] * mixed_ref[h]).astype(BF16)
        grad_ref[h] = grad
        sum_ref[1, h] = dot(squery_ref[h], grad, TN)

    for h in turn:
        grad_sum(other + h)
        core_copy(1, h).start()
    for n in range(own_count):
        grad_sum(own + turn[n])
        send_up(1, 1 - core, n)

    def inner_grads(h, carry):
        cols = head_cols(h)
        grad = grad_ref[h]
        back = (dot(grad, v_ref[:, cols], NT) * weight_ref[h]).astype(BF16)
        dq = dot(back, k_ref[:, cols], NN) + dot(grad, low_ref[0, h], NT) * decay_query(h)
        dq_ref[:, cols] = dq.astype(BF16)
        dkp_ref[h] = dot(back, q_ref[:, cols], TN)
        dvp_ref[h] = dot(attend_ref[h], grad, TN)
        return carry

    lax.fori_loop(0, heads, inner_grads, 0)

    scan_and_send_down(1)

    def outer_grads(h):
        cols = head_cols(h)
        decay = decay_key(h)
        low = low_ref[1, h]
        dk_ref[:, cols] = (dkp_ref[h] + dot(v_ref[:, cols], low, NT) * decay).astype(BF16)
        dv_ref[:, cols] = (dvp_ref[h] + dot(k_ref[:, cols], low, NN) * decay).astype(BF16)

    deliver(1, 1 - core, outer_grads)

    log_copy.wait_send()
    for oy in range(1, ny):
        sums_copy(oy).wait_send()
    for ox, oz in offsets:
        rate_copy(ox, oz).wait_send()
    for way in range(2):
        for i in range(own_count):
            core_copy(way, i).wait_send()
            give_copy(way, i).wait_send()
        for ox, oz in offsets:
            up_copy(way, ox, oz).wait_send()
            down_copy(way, ox, oz).wait_send()


def hand_over(dq_ref, dk_ref, dv_ref, dq_out, dk_out, dv_out, sems):
    copies = [
        pltpu.make_async_copy(src, dst, sems.at[n])
        for n, (src, dst) in enumerate([(dq_ref, dq_out), (dk_ref, dk_out), (dv_ref, dv_out)])
    ]
    for copy in copies:
        copy.start()
    for copy in copies:
        copy.wait()


def body(queries, key_rows, value_rows, log_decay, out_grad, norm_gain):
    length, width = queries.shape
    heads = width // DIM
    ny = lax.axis_size("head")
    chips = lax.axis_size("ctx") // 2
    nx = heads // 2
    nz = chips // nx
    half = heads // 2
    rows = DIM // nz
    out = jax.ShapeDtypeStruct((length, width), BF16)
    vmem = pl.BlockSpec(memory_space=pltpu.VMEM)
    dma = pltpu.SemaphoreType.DMA
    hbm = pl.BlockSpec(memory_space=pl.ANY)
    inner = pltpu.VMEM((length, width), BF16)
    grads = pl.pallas_call(
        functools.partial(kernel, heads, nx, nz, ny),
        out_shape=(inner, inner, inner),
        in_specs=[hbm] * 6,
        out_specs=(vmem, vmem, vmem),
        scratch_shapes=[
            pltpu.VMEM((length, width), BF16),
            pltpu.VMEM((length, width), BF16),
            pltpu.VMEM((length, width), BF16),
            pltpu.VMEM((heads, BLOCK), F32),
            pltpu.VMEM((length, width), BF16),
            pltpu.VMEM((heads, DIM), F32),
            pltpu.VMEM((heads, BLOCK, DIM), F32),
            pltpu.VMEM((heads, BLOCK), F32),
            pltpu.VMEM((heads, 1, DIM), F32),
            pltpu.VMEM((heads, 1, DIM), F32),
            pltpu.VMEM((half, 1, DIM), F32),
            pltpu.VMEM((chips, 1, DIM), F32),
            pltpu.VMEM((chips, 1, DIM), F32),
            pltpu.VMEM((heads, BLOCK, BLOCK), F32),
            pltpu.VMEM((heads, BLOCK, BLOCK), BF16),
            pltpu.VMEM((heads, BLOCK, DIM), F32),
            pltpu.VMEM((heads, BLOCK, DIM), BF16),
            pltpu.VMEM((heads, BLOCK, DIM), BF16),
            pltpu.VMEM((heads, BLOCK, DIM), F32),
            pltpu.VMEM((heads, BLOCK, DIM), F32),
            pltpu.VMEM((BLOCK, DIM), F32),
            pltpu.VMEM((BLOCK, DIM), F32),
            pltpu.VMEM((8, BLOCK), F32),
            pltpu.VMEM((ny, 8, BLOCK), F32),
            pltpu.VMEM((2, heads, DIM, DIM), F32),
            pltpu.VMEM((2, half, DIM, DIM), F32),
            pltpu.VMEM((2, half, DIM, DIM), F32),
            pltpu.VMEM((2, chips, rows, DIM), F32),
            pltpu.VMEM((2, chips, rows, DIM), F32),
            pltpu.VMEM((2, half, DIM, DIM), F32),
            pltpu.VMEM((2, half, DIM, DIM), F32),
            pltpu.VMEM((2, half, DIM, DIM), F32),
            pltpu.VMEM((2, heads, DIM, DIM), BF16),
            dma((6,)),
            dma((chips + 1,)),
            dma((chips + 1,)),
            dma((ny,)),
            dma((ny,)),
            dma((2, half)),
            dma((2, half)),
            dma((2, chips)),
            dma((2, chips)),
            dma((2, chips)),
            dma((2, chips)),
            dma((2, half)),
            dma((2, half)),
        ],
        compiler_params=pltpu.CompilerParams(
            collective_id=0, has_side_effects=True, vmem_limit_bytes=60 * 2**20
        ),
        name="lightning",
    )(
        queries, key_rows, value_rows, log_decay, out_grad,
        norm_gain.reshape(heads, DIM),
    )
    return pl.pallas_call(
        hand_over,
        out_shape=(out, out, out),
        in_specs=[vmem] * 3,
        out_specs=(hbm, hbm, hbm),
        scratch_shapes=[dma((3,))],
        name="hand_over",
    )(*(pltpu.with_memory_space_constraint(x, pltpu.VMEM) for x in grads))


def solution(mesh):
    return jax.shard_map(
        body,
        mesh=mesh,
        in_specs=(
            P("ctx", "head"),
            P("ctx", "head"),
            P("ctx", "head"),
            P("head", "ctx"),
            P("ctx", "head"),
            P("head"),
        ),
        out_specs=(P("ctx", "head"), P("ctx", "head"), P("ctx", "head")),
        check_vma=False,
    )
```

```python
import functools

import jax
import jax.numpy as jnp
from jax import lax
from jax.experimental import pallas as pl
from jax.experimental.pallas import tpu as pltpu
from jax.sharding import PartitionSpec as P

DIM = 128
BLOCK = 256
F32 = jnp.float32
BF16 = jnp.bfloat16
HIGH = lax.Precision.HIGHEST
NN = (((1,), (0,)), ((), ()))
NT = (((1,), (1,)), ((), ()))
TN = (((0,), (0,)), ((), ()))


def dot(a, b, dims, precision=None):
    return lax.dot_general(a, b, dims, precision=precision, preferred_element_type=F32)


def ring_order(count):
    return sorted(range(count), key=lambda step: (-min(step, count - step), step))


def split3(x, axis):
    high = x.astype(BF16)
    rest = x - high.astype(F32)
    middle = rest.astype(BF16)
    low = (rest - middle.astype(F32)).astype(BF16)
    return jnp.concatenate([high, middle, low], axis=axis)


def kernel(
    heads, nx, nz, ny,
    q_hbm, k_hbm, v_hbm, ld_hbm, og_hbm, gain_hbm,
    dq_ref, dk_ref, dv_ref,
    q_ref, k_ref, v_ref, ld_ref, og_ref, gain_ref,
    col_ref, cum_ref, end_ref, pend_ref, lrep_ref, lin_ref, rate_ref,
    weight_ref, attend_ref, mixed_ref, grad_ref, squery_ref, dkp_ref, dvp_ref,
    power_ref, align_ref, red_ref, yin_ref,
    sum_ref, srecv_ref, schip_ref, sin_ref, pout_ref, pin_ref, give_ref, erecv_ref, low_ref,
    in_sem, ls_sem, lr_sem, ys_sem, yr_sem,
    cs_sem, cr_sem, us_sem, ur_sem, ds_sem, dr_sem, es_sem, er_sem,
):
    chips = nx * nz
    own_count = heads // 2
    rows = DIM // nz
    ctx = lax.axis_index("ctx")
    yy = lax.axis_index("head")
    core = lax.rem(ctx, 2)
    chip = lax.div(ctx, 2)
    mx = lax.div(chip, nz)
    mz = lax.rem(chip, nz)
    own = own_count * core
    other = own_count * (1 - core)
    partner = {"ctx": 2 * chip + (1 - core)}
    xs = ring_order(nx)
    zs = ring_order(nz)
    px = [lax.rem(mx + o, nx) for o in range(nx)]
    pz = [lax.rem(mz + o, nz) for o in range(nz)]
    index_of = [[px[ox] * nz + pz[oz] for oz in range(nz)] for ox in range(nx)]
    offsets = [(ox, oz) for ox in xs for oz in zs if (ox, oz) != (0, 0)]
    turn = [px[ox] for ox in xs]

    def chip_id(index):
        return {"ctx": 2 * index + core}

    def remote(src, dst, send, recv, device):
        return pltpu.make_async_remote_copy(
            src_ref=src, dst_ref=dst, send_sem=send, recv_sem=recv,
            device_id=device, device_id_type=pl.DeviceIdType.MESH,
        )

    barrier = pltpu.get_barrier_semaphore()

    def greet(device):
        pl.semaphore_signal(
            barrier, inc=1, device_id=device, device_id_type=pl.DeviceIdType.MESH
        )

    for ox, oz in offsets:
        greet(chip_id(index_of[ox][oz]))
    greet(partner)
    for oy in range(1, ny):
        greet({"head": lax.rem(yy + oy, ny)})

    loads = [
        pltpu.make_async_copy(src, dst, in_sem.at[n])
        for n, (src, dst) in enumerate(
            [
                (ld_hbm, ld_ref), (k_hbm, k_ref), (v_hbm, v_ref),
                (q_hbm, q_ref), (og_hbm, og_ref), (gain_hbm, gain_ref),
            ]
        )
    ]
    for load in loads:
        load.start()

    def head_cols(h):
        return pl.ds(pl.multiple_of(h * DIM, DIM), DIM)

    step_u = lax.broadcasted_iota(jnp.int32, (BLOCK, BLOCK), 0)
    step_t = lax.broadcasted_iota(jnp.int32, (BLOCK, BLOCK), 1)
    loads[0].wait()
    cum = dot(ld_ref[...], (step_u <= step_t).astype(F32), NN, HIGH)
    cum_ref[...] = cum
    pick = lax.broadcasted_iota(jnp.int32, (heads, DIM), 0)
    for h in range(heads):
        col = dot(cum, (pick == h).astype(F32), TN, HIGH)
        col_ref[h] = col
        end_ref[h] = col[BLOCK - 1 : BLOCK, :]
    loads[1].wait()
    loads[2].wait()

    def decay_key(h):
        return jnp.exp(end_ref[h] - col_ref[h])

    def decay_query(h):
        return jnp.exp(col_ref[h])

    def key_sum(i, base):
        h = base + i
        keyed = (k_ref[:, head_cols(h)].astype(F32) * decay_key(h)).astype(BF16)
        sum_ref[0, h] = dot(keyed, v_ref[:, head_cols(h)], TN)
        return base

    def core_copy(way, i):
        return remote(
            sum_ref.at[way, other + i], srecv_ref.at[way, i],
            cs_sem.at[way, i], cr_sem.at[way, i], partner,
        )

    log_copy = remote(end_ref, pend_ref, ls_sem.at[1], lr_sem.at[1], partner)

    lax.fori_loop(0, own_count, key_sum, other)
    lax.fori_loop(0, own_count, key_sum, own)
    loads[3].wait()

    pl.semaphore_wait(barrier, chips - 1 + 1 + ny - 1)

    log_copy.start()
    for h in turn:
        core_copy(0, h).start()

    log_copy.wait_recv()
    for i in range(own_count):
        lrep_ref[i] = end_ref[own + i] + pend_ref[own + i]

    def rate_copy(ox, oz):
        index = index_of[ox][oz]
        return remote(
            lrep_ref.at[px[ox]], lin_ref.at[chip], ls_sem.at[0], lr_sem.at[0],
            chip_id(index),
        )

    lin_most = lin_ref.at[pl.ds(0, chips - 1)]
    rate_all = remote(lin_most, lin_most, ls_sem.at[0], lr_sem.at[0], partner)

    def up_copy(way, ox, oz):
        index = index_of[ox][oz]
        return remote(
            schip_ref.at[way, px[ox], pl.ds(pl.multiple_of(pz[oz] * rows, rows), rows)],
            sin_ref.at[way, chip],
            us_sem.at[way], ur_sem.at[way], chip_id(index),
        )

    def up_all(way):
        most = sin_ref.at[way, pl.ds(0, chips - 1)]
        return remote(most, most, us_sem.at[way], ur_sem.at[way], partner)

    my_rows = pl.ds(pl.multiple_of(mz * rows, rows), rows)

    def down_copy(way, ox, oz):
        index = index_of[ox][oz]
        return remote(
            pout_ref.at[way, index], pin_ref.at[way, mx, my_rows],
            ds_sem.at[way], dr_sem.at[way, mx], chip_id(index),
        )

    def down_all(way):
        most = pout_ref.at[way, pl.ds(0, chips - 1)]
        return remote(most, most, ds_sem.at[way], dr_sem.at[way, 0], partner)

    def down_head(way, ox):
        whole = pin_ref.at[way, px[ox], pl.ds(0, DIM if ox else DIM - rows)]
        return remote(whole, whole, ds_sem.at[way], dr_sem.at[way, px[ox]], partner)

    def give_copy(way, h):
        return remote(
            give_ref.at[way, h], erecv_ref.at[way, h],
            es_sem.at[way, h], er_sem.at[way, h], partner,
        )

    one = jnp.ones((1, DIM), F32)
    none = jnp.zeros((1, DIM), F32)

    def send_up(way, cc, n):
        ox, h = xs[n], turn[n]
        core_copy(way, h).wait_recv()
        mine = jnp.where(cc == 0, jnp.exp(pend_ref[own + h]), one)
        theirs = jnp.where(cc == 0, one, jnp.exp(end_ref[own + h]))
        schip_ref[way, h] = mine * sum_ref[way, own + h] + theirs * srecv_ref[way, h]
        for oz in zs:
            if (ox, oz) != (0, 0):
                up_copy(way, ox, oz).start()
            else:
                sin_ref[way, chip] = schip_ref[way, mx, my_rows, :]

    def scan_and_send_down(way):
        up_all(way).wait_recv()

        def advance(step, carry):
            index = step if way == 0 else chips - 1 - step
            pout_ref[way, index] = carry
            return rate_ref[index] * carry + sin_ref[way, index]

        lax.fori_loop(0, chips, advance, jnp.zeros((rows, DIM), F32), unroll=8)
        for ox, oz in offsets:
            down_copy(way, ox, oz).start()
        pin_ref[way, mx, my_rows, :] = pout_ref[way, chip]

    def take_own(way, cc, n):
        ox, h = xs[n], turn[n]
        down_head(way, ox).wait_recv()
        before = pin_ref[way, h]
        give_ref[way, h] = (
            jnp.where(cc == 0, jnp.exp(end_ref[own + h]), one) * before
            + jnp.where(cc == 0, one, none) * sum_ref[way, own + h]
        )
        give_copy(way, h).start()
        low_ref[way, own + h] = (
            jnp.where(cc == 0, one, jnp.exp(pend_ref[own + h])) * before
            + jnp.where(cc == 0, none, one) * srecv_ref[way, h]
        ).astype(BF16)

    def take_other(way, n):
        h = turn[n]
        give_copy(way, h).wait_recv()
        low_ref[way, other + h] = erecv_ref[way, h].astype(BF16)

    def deliver(way, cc, use):
        for n in range(own_count):
            take_own(way, cc, n)
            if n > 1:
                take_other(way, n - 2)
                use(other + turn[n - 2])
            use(own + turn[n])
        for n in range(own_count - 2, own_count):
            take_other(way, n)
            use(other + turn[n])

    for ox, oz in offsets:
        rate_copy(ox, oz).start()
    lin_ref[chip] = lrep_ref[mx]
    for n in range(own_count):
        send_up(0, core, n)

    lower = step_t <= step_u

    def inner_out(h, carry):
        col = col_ref[h]
        gap = jnp.concatenate([col, col], axis=1) - cum_ref[pl.ds(h, 1), :]
        weight = jnp.where(lower, jnp.exp(jnp.where(lower, gap, 0.0)), 0.0)
        weight_ref[h] = weight
        q = q_ref[:, head_cols(h)]
        attend = (dot(q, k_ref[:, head_cols(h)], NT) * weight).astype(BF16)
        attend_ref[h] = attend
        mixed_ref[h] = dot(attend, v_ref[:, head_cols(h)], NN)
        squery_ref[h] = (q.astype(F32) * decay_query(h)).astype(BF16)
        return carry

    lax.fori_loop(0, heads, inner_out, 0)
    loads[4].wait()
    loads[5].wait()
    power_ref[...] = jnp.zeros_like(power_ref)
    align_ref[...] = jnp.zeros_like(align_ref)

    rate_all.wait_recv()
    rate_ref[...] = jnp.exp(lin_ref[...])

    scan_and_send_down(0)

    def scaled_grad(h):
        return og_ref[:, head_cols(h)].astype(F32) * gain_ref[pl.ds(h, 1), :]

    def outer_out(h):
        mixed = mixed_ref[h] + dot(q_ref[:, head_cols(h)], low_ref[0, h], NN) * decay_query(h)
        mixed_ref[h] = mixed
        power_ref[...] += mixed * mixed
        align_ref[...] += scaled_grad(h) * mixed

    deliver(0, core, outer_out)

    ones = jnp.ones((8, 3 * DIM), BF16)
    sums_row = lax.broadcasted_iota(jnp.int32, (8, BLOCK), 0)
    red_ref[...] = jnp.where(
        sums_row < 4,
        dot(ones, split3(power_ref[...], 1), NT),
        dot(ones, split3(align_ref[...], 1), NT),
    )

    def sums_copy(oy):
        to = lax.rem(yy + oy, ny)
        return remote(red_ref, yin_ref.at[yy], ys_sem.at[0], yr_sem.at[0], {"head": to})

    yin_most = yin_ref.at[pl.ds(0, ny - 1)]
    sums_all = remote(yin_most, yin_most, ys_sem.at[0], yr_sem.at[0], partner)

    for oy in range(1, ny):
        sums_copy(oy).start()
    yin_ref[yy] = red_ref[...]
    sums_all.wait_recv()
    total = yin_ref[0]
    for index in range(1, ny):
        total = total + yin_ref[index]
    features = heads * DIM * ny
    inverse = lax.rsqrt(total[0:1, :] / features + 1e-6)
    factor = inverse * inverse * inverse * (total[4:5, :] / features)
    pair_row = lax.broadcasted_iota(jnp.int32, (16, BLOCK), 0)
    pair = split3(jnp.where(pair_row < 8, inverse, factor), 0)
    pick_row = lax.rem(lax.broadcasted_iota(jnp.int32, (48, DIM), 0), 16)
    inverse_col = dot(pair, jnp.where(pick_row == 0, 1.0, 0.0).astype(BF16), TN)
    factor_col = dot(pair, jnp.where(pick_row == 8, 1.0, 0.0).astype(BF16), TN)
    power_ref[...] = inverse_col
    align_ref[...] = factor_col

    def grad_sum(h):
        grad = (power_ref[...] * scaled_grad(h) - align_ref[...] * mixed_ref[h]).astype(BF16)
        grad_ref[h] = grad
        sum_ref[1, h] = dot(squery_ref[h], grad, TN)

    for h in turn:
        grad_sum(other + h)
        core_copy(1, h).start()
    for n in range(own_count):
        grad_sum(own + turn[n])
        send_up(1, 1 - core, n)

    def inner_grads(h, carry):
        cols = head_cols(h)
        grad = grad_ref[h]
        back = (dot(grad, v_ref[:, cols], NT) * weight_ref[h]).astype(BF16)
        dq = dot(back, k_ref[:, cols], NN) + dot(grad, low_ref[0, h], NT) * decay_query(h)
        dq_ref[:, cols] = dq.astype(BF16)
        dkp_ref[h] = dot(back, q_ref[:, cols], TN)
        dvp_ref[h] = dot(attend_ref[h], grad, TN)
        return carry

    lax.fori_loop(0, heads, inner_grads, 0)

    scan_and_send_down(1)

    def outer_grads(h):
        cols = head_cols(h)
        decay = decay_key(h)
        low = low_ref[1, h]
        dk_ref[:, cols] = (dkp_ref[h] + dot(v_ref[:, cols], low, NT) * decay).astype(BF16)
        dv_ref[:, cols] = (dvp_ref[h] + dot(k_ref[:, cols], low, NN) * decay).astype(BF16)

    deliver(1, 1 - core, outer_grads)

    log_copy.wait_send()
    sums_all.wait_send()
    rate_all.wait_send()
    for way in range(2):
        for i in range(own_count):
            core_copy(way, i).wait_send()
            give_copy(way, i).wait_send()
        up_all(way).wait_send()
        down_all(way).wait_send()


def hand_over(dq_ref, dk_ref, dv_ref, dq_out, dk_out, dv_out, sems):
    copies = [
        pltpu.make_async_copy(src, dst, sems.at[n])
        for n, (src, dst) in enumerate([(dq_ref, dq_out), (dk_ref, dk_out), (dv_ref, dv_out)])
    ]
    for copy in copies:
        copy.start()
    for copy in copies:
        copy.wait()


def body(queries, key_rows, value_rows, log_decay, out_grad, norm_gain):
    length, width = queries.shape
    heads = width // DIM
    ny = lax.axis_size("head")
    chips = lax.axis_size("ctx") // 2
    nx = heads // 2
    nz = chips // nx
    half = heads // 2
    rows = DIM // nz
    out = jax.ShapeDtypeStruct((length, width), BF16)
    vmem = pl.BlockSpec(memory_space=pltpu.VMEM)
    dma = pltpu.SemaphoreType.DMA
    hbm = pl.BlockSpec(memory_space=pl.ANY)
    inner = pltpu.VMEM((length, width), BF16)
    grads = pl.pallas_call(
        functools.partial(kernel, heads, nx, nz, ny),
        out_shape=(inner, inner, inner),
        in_specs=[hbm] * 6,
        out_specs=(vmem, vmem, vmem),
        scratch_shapes=[
            pltpu.VMEM((length, width), BF16),
            pltpu.VMEM((length, width), BF16),
            pltpu.VMEM((length, width), BF16),
            pltpu.VMEM((heads, BLOCK), F32),
            pltpu.VMEM((length, width), BF16),
            pltpu.VMEM((heads, DIM), F32),
            pltpu.VMEM((heads, BLOCK, DIM), F32),
            pltpu.VMEM((heads, BLOCK), F32),
            pltpu.VMEM((heads, 1, DIM), F32),
            pltpu.VMEM((heads, 1, DIM), F32),
            pltpu.VMEM((half, 1, DIM), F32),
            pltpu.VMEM((chips, 1, DIM), F32),
            pltpu.VMEM((chips, 1, DIM), F32),
            pltpu.VMEM((heads, BLOCK, BLOCK), F32),
            pltpu.VMEM((heads, BLOCK, BLOCK), BF16),
            pltpu.VMEM((heads, BLOCK, DIM), F32),
            pltpu.VMEM((heads, BLOCK, DIM), BF16),
            pltpu.VMEM((heads, BLOCK, DIM), BF16),
            pltpu.VMEM((heads, BLOCK, DIM), F32),
            pltpu.VMEM((heads, BLOCK, DIM), F32),
            pltpu.VMEM((BLOCK, DIM), F32),
            pltpu.VMEM((BLOCK, DIM), F32),
            pltpu.VMEM((8, BLOCK), F32),
            pltpu.VMEM((ny, 8, BLOCK), F32),
            pltpu.VMEM((2, heads, DIM, DIM), F32),
            pltpu.VMEM((2, half, DIM, DIM), F32),
            pltpu.VMEM((2, half, DIM, DIM), F32),
            pltpu.VMEM((2, chips, rows, DIM), F32),
            pltpu.VMEM((2, chips, rows, DIM), F32),
            pltpu.VMEM((2, half, DIM, DIM), F32),
            pltpu.VMEM((2, half, DIM, DIM), F32),
            pltpu.VMEM((2, half, DIM, DIM), F32),
            pltpu.VMEM((2, heads, DIM, DIM), BF16),
            dma((6,)),
            dma((2,)),
            dma((2,)),
            dma((1,)),
            dma((1,)),
            dma((2, half)),
            dma((2, half)),
            dma((2,)),
            dma((2,)),
            dma((2,)),
            dma((2, nx)),
            dma((2, half)),
            dma((2, half)),
        ],
        compiler_params=pltpu.CompilerParams(
            collective_id=0, has_side_effects=True, vmem_limit_bytes=60 * 2**20
        ),
        name="lightning",
    )(
        queries, key_rows, value_rows, log_decay, out_grad,
        norm_gain.reshape(heads, DIM),
    )
    return pl.pallas_call(
        hand_over,
        out_shape=(out, out, out),
        in_specs=[vmem] * 3,
        out_specs=(hbm, hbm, hbm),
        scratch_shapes=[dma((3,))],
        name="hand_over",
    )(*(pltpu.with_memory_space_constraint(x, pltpu.VMEM) for x in grads))


def solution(mesh):
    return jax.shard_map(
        body,
        mesh=mesh,
        in_specs=(
            P("ctx", "head"),
            P("ctx", "head"),
            P("ctx", "head"),
            P("head", "ctx"),
            P("ctx", "head"),
            P("head"),
        ),
        out_specs=(P("ctx", "head"), P("ctx", "head"), P("ctx", "head")),
        check_vma=False,
    )
```

```python
import functools

import jax
import jax.numpy as jnp
from jax import lax
from jax.experimental import pallas as pl
from jax.experimental.pallas import tpu as pltpu
from jax.sharding import PartitionSpec as P

DIM = 128
BLOCK = 256
F32 = jnp.float32
BF16 = jnp.bfloat16
HIGH = lax.Precision.HIGHEST
NN = (((1,), (0,)), ((), ()))
NT = (((1,), (1,)), ((), ()))
TN = (((0,), (0,)), ((), ()))


def dot(a, b, dims, precision=None):
    return lax.dot_general(a, b, dims, precision=precision, preferred_element_type=F32)


def ring_order(count):
    return sorted(range(count), key=lambda step: (-min(step, count - step), step))


def split3(x, axis):
    high = x.astype(BF16)
    rest = x - high.astype(F32)
    middle = rest.astype(BF16)
    low = (rest - middle.astype(F32)).astype(BF16)
    return jnp.concatenate([high, middle, low], axis=axis)


def kernel(
    heads, nx, nz, ny,
    q_hbm, k_hbm, v_hbm, ld_hbm, og_hbm, gain_hbm,
    dq_ref, dk_ref, dv_ref,
    q_ref, k_ref, v_ref, ld_ref, og_ref, gain_ref,
    col_ref, cum_ref, end_ref, pend_ref, lrep_ref, lin_ref, rate_ref,
    weight_ref, attend_ref, mixed_ref, grad_ref, squery_ref, dkp_ref, dvp_ref,
    qdecay_ref, kdecay_ref, power_ref, align_ref, red_ref, yin_ref,
    sum_ref, srecv_ref, schip_ref, sin_ref, pout_ref, pin_ref, give_ref, erecv_ref, low_ref,
    in_sem, ls_sem, lr_sem, ys_sem, yr_sem,
    cs_sem, cr_sem, us_sem, ur_sem, ds_sem, dr_sem, es_sem, er_sem,
):
    chips = nx * nz
    own_count = heads // 2
    phase_heads = own_count // 2
    share = nx // phase_heads
    rows = DIM // (share * nz)
    ctx = lax.axis_index("ctx")
    yy = lax.axis_index("head")
    core = lax.rem(ctx, 2)
    chip = lax.div(ctx, 2)
    mx = lax.div(chip, nz)
    mz = lax.rem(chip, nz)
    own = own_count * core
    other = own_count * (1 - core)
    partner = {"ctx": 2 * chip + (1 - core)}
    px = [lax.rem(mx + o, nx) for o in range(nx)]
    pz = [lax.rem(mz + o, nz) for o in range(nz)]
    index_of = [[px[ox] * nz + pz[oz] for oz in range(nz)] for ox in range(nx)]
    offsets = sorted(
        [(ox, oz) for ox in ring_order(nx) for oz in ring_order(nz) if (ox, oz) != (0, 0)],
        key=lambda o: -(min(o[0], nx - o[0]) + min(o[1], nz - o[1])),
    )
    seat = [lax.div(x, share) for x in px]
    lane = [lax.rem(x, share) * nz for x in px]

    def chip_id(index):
        return {"ctx": 2 * index + core}

    def remote(src, dst, send, recv, device):
        return pltpu.make_async_remote_copy(
            src_ref=src, dst_ref=dst, send_sem=send, recv_sem=recv,
            device_id=device, device_id_type=pl.DeviceIdType.MESH,
        )

    barrier = pltpu.get_barrier_semaphore()

    def greet(device):
        pl.semaphore_signal(
            barrier, inc=1, device_id=device, device_id_type=pl.DeviceIdType.MESH
        )

    for ox, oz in offsets:
        greet(chip_id(index_of[ox][oz]))
    greet(partner)
    for oy in range(1, ny):
        greet({"head": lax.rem(yy + oy, ny)})

    loads = [
        pltpu.make_async_copy(src, dst, in_sem.at[n])
        for n, (src, dst) in enumerate(
            [
                (ld_hbm, ld_ref), (k_hbm, k_ref), (v_hbm, v_ref),
                (q_hbm, q_ref), (og_hbm, og_ref), (gain_hbm, gain_ref),
            ]
        )
    ]
    for load in loads:
        load.start()

    def head_cols(h):
        return pl.ds(pl.multiple_of(h * DIM, DIM), DIM)

    step_u = lax.broadcasted_iota(jnp.int32, (BLOCK, BLOCK), 0)
    step_t = lax.broadcasted_iota(jnp.int32, (BLOCK, BLOCK), 1)
    loads[0].wait()
    cum = dot(ld_ref[...], (step_u <= step_t).astype(F32), NN, HIGH)
    cum_ref[...] = cum
    pick = lax.broadcasted_iota(jnp.int32, (heads, DIM), 0)
    for h in range(heads):
        col = dot(cum, (pick == h).astype(F32), TN, HIGH)
        col_ref[h] = col
        end_ref[h] = col[BLOCK - 1 : BLOCK, :]
    loads[1].wait()
    loads[2].wait()

    def key_sum(i, base):
        h = base + i
        decay = jnp.exp(end_ref[h] - col_ref[h])
        kdecay_ref[h] = decay
        keyed = (k_ref[:, head_cols(h)].astype(F32) * decay).astype(BF16)
        sum_ref[0, h] = dot(keyed, v_ref[:, head_cols(h)], TN)
        return base

    def core_copy(way, i):
        return remote(
            sum_ref.at[way, other + i], srecv_ref.at[way, i],
            cs_sem.at[way], cr_sem.at[way, i], partner,
        )

    log_copy = remote(end_ref, pend_ref, ls_sem.at[1], lr_sem.at[1], partner)

    lax.fori_loop(0, own_count, key_sum, other)
    lax.fori_loop(0, own_count, key_sum, own)
    loads[3].wait()

    pl.semaphore_wait(barrier, chips - 1 + 1 + ny - 1)

    log_copy.start()
    for h in range(own_count):
        core_copy(0, h).start()

    log_copy.wait_recv()
    for p in range(2):
        for j in range(phase_heads):
            i = own + phase_heads * p + j
            lrep_ref[j, p] = end_ref[i] + pend_ref[i]

    def rate_copy(ox, oz):
        index = index_of[ox][oz]
        return remote(
            lrep_ref.at[seat[ox]], lin_ref.at[chip], ls_sem.at[0], lr_sem.at[0],
            chip_id(index),
        )

    lin_most = lin_ref.at[pl.ds(0, chips - 1)]
    rate_all = remote(lin_most, lin_most, ls_sem.at[0], lr_sem.at[0], partner)

    def slice_of(ox, oz):
        return pl.ds(pl.multiple_of((lane[ox] + pz[oz]) * rows, rows), rows)

    def up_copy(way, p, ox, oz):
        index = index_of[ox][oz]
        return remote(
            schip_ref.at[way, phase_heads * p + seat[ox], slice_of(ox, oz)],
            sin_ref.at[way, p, chip],
            us_sem.at[way], ur_sem.at[way, p], chip_id(index),
        )

    def up_all(way, p):
        most = sin_ref.at[way, p, pl.ds(0, chips - 1)]
        return remote(most, most, us_sem.at[way], ur_sem.at[way, p], partner)

    def down_copy(way, p, ox, oz):
        index = index_of[ox][oz]
        return remote(
            pout_ref.at[way, p, index],
            pin_ref.at[way, phase_heads * p + seat[0], slice_of(0, 0)],
            ds_sem.at[way], dr_sem.at[way, p], chip_id(index),
        )

    def down_all(way, p):
        most = pout_ref.at[way, p, pl.ds(0, chips - 1)]
        return remote(most, most, ds_sem.at[way], dr_sem.at[way, p], partner)

    def sent_all(way):
        up = sin_ref.at[way, pl.ds(0, 2), pl.ds(0, chips - 1)]
        down = pout_ref.at[way, pl.ds(0, 2), pl.ds(0, chips - 1)]
        return (
            remote(up, up, us_sem.at[way], ur_sem.at[way, 0], partner),
            remote(down, down, ds_sem.at[way], dr_sem.at[way, 0], partner),
        )

    def give_copy(way, h):
        return remote(
            give_ref.at[way, h], erecv_ref.at[way, h],
            es_sem.at[way], er_sem.at[way, h], partner,
        )

    one = jnp.ones((1, DIM), F32)
    none = jnp.zeros((1, DIM), F32)

    def phase(p):
        return range(phase_heads * p, phase_heads * (p + 1))

    def send_up(way, cc, p):
        for h in phase(p):
            core_copy(way, h).wait_recv()
            mine = jnp.where(cc == 0, jnp.exp(pend_ref[own + h]), one)
            theirs = jnp.where(cc == 0, one, jnp.exp(end_ref[own + h]))
            schip_ref[way, h] = mine * sum_ref[way, own + h] + theirs * srecv_ref[way, h]
        for ox, oz in offsets:
            up_copy(way, p, ox, oz).start()
        sin_ref[way, p, chip] = schip_ref[way, phase_heads * p + seat[0], slice_of(0, 0), :]

    def scan_and_send_down(way, p):
        up_all(way, p).wait_recv()

        def advance(step, carry):
            index = step if way == 0 else chips - 1 - step
            pout_ref[way, p, index] = carry
            return rate_ref[index, p] * carry + sin_ref[way, p, index]

        lax.fori_loop(0, chips, advance, jnp.zeros((rows, DIM), F32), unroll=8)
        for ox, oz in offsets:
            down_copy(way, p, ox, oz).start()
        pin_ref[way, phase_heads * p + seat[0], slice_of(0, 0), :] = pout_ref[way, p, chip]

    def take_own(way, cc, h):
        before = pin_ref[way, h]
        give_ref[way, h] = (
            jnp.where(cc == 0, jnp.exp(end_ref[own + h]), one) * before
            + jnp.where(cc == 0, one, none) * sum_ref[way, own + h]
        )
        give_copy(way, h).start()
        low_ref[way, own + h] = (
            jnp.where(cc == 0, one, jnp.exp(pend_ref[own + h])) * before
            + jnp.where(cc == 0, none, one) * srecv_ref[way, h]
        ).astype(BF16)

    def take_other(way, h):
        give_copy(way, h).wait_recv()
        low_ref[way, other + h] = erecv_ref[way, h].astype(BF16)

    def deliver(way, cc, use):
        for p in range(2):
            down_all(way, p).wait_recv()
            for h in phase(p):
                take_own(way, cc, h)
            for h in phase(p):
                use(own + h)
            for h in phase(p):
                take_other(way, h)
                use(other + h)

    send_up(0, core, 0)
    for ox, oz in offsets:
        rate_copy(ox, oz).start()
    lin_ref[chip] = lrep_ref[seat[0]]
    send_up(0, core, 1)

    lower = step_t <= step_u

    def inner_out(h, carry):
        col = col_ref[h]
        gap = jnp.concatenate([col, col], axis=1) - cum_ref[pl.ds(h, 1), :]
        weight = jnp.where(lower, jnp.exp(jnp.where(lower, gap, 0.0)), 0.0)
        weight_ref[h] = weight
        q = q_ref[:, head_cols(h)]
        attend = (dot(q, k_ref[:, head_cols(h)], NT) * weight).astype(BF16)
        attend_ref[h] = attend
        mixed_ref[h] = dot(attend, v_ref[:, head_cols(h)], NN)
        decay = jnp.exp(col)
        qdecay_ref[h] = decay
        squery_ref[h] = (q.astype(F32) * decay).astype(BF16)
        return carry

    lax.fori_loop(0, heads, inner_out, 0)
    loads[4].wait()
    loads[5].wait()
    power_ref[...] = jnp.zeros_like(power_ref)
    align_ref[...] = jnp.zeros_like(align_ref)

    rate_all.wait_recv()
    rate_ref[...] = jnp.exp(lin_ref[...])

    scan_and_send_down(0, 0)
    scan_and_send_down(0, 1)

    def scaled_grad(h):
        return og_ref[:, head_cols(h)].astype(F32) * gain_ref[pl.ds(h, 1), :]

    def outer_out(h):
        mixed = mixed_ref[h] + dot(q_ref[:, head_cols(h)], low_ref[0, h], NN) * qdecay_ref[h]
        mixed_ref[h] = mixed
        power_ref[...] += mixed * mixed
        align_ref[...] += scaled_grad(h) * mixed

    deliver(0, core, outer_out)

    ones = jnp.ones((8, 3 * DIM), BF16)
    sums_row = lax.broadcasted_iota(jnp.int32, (8, BLOCK), 0)
    red_ref[...] = jnp.where(
        sums_row < 4,
        dot(ones, split3(power_ref[...], 1), NT),
        dot(ones, split3(align_ref[...], 1), NT),
    )

    def sums_copy(oy):
        to = lax.rem(yy + oy, ny)
        return remote(red_ref, yin_ref.at[yy], ys_sem.at[0], yr_sem.at[0], {"head": to})

    yin_most = yin_ref.at[pl.ds(0, ny - 1)]
    sums_all = remote(yin_most, yin_most, ys_sem.at[0], yr_sem.at[0], partner)

    for oy in range(1, ny):
        sums_copy(oy).start()
    yin_ref[yy] = red_ref[...]
    sums_all.wait_recv()
    total = yin_ref[0]
    for index in range(1, ny):
        total = total + yin_ref[index]
    features = heads * DIM * ny
    inverse = lax.rsqrt(total[0:1, :] / features + 1e-6)
    factor = inverse * inverse * inverse * (total[4:5, :] / features)
    pair_row = lax.broadcasted_iota(jnp.int32, (16, BLOCK), 0)
    pair = split3(jnp.where(pair_row < 8, inverse, factor), 0)
    pick_row = lax.rem(lax.broadcasted_iota(jnp.int32, (48, DIM), 0), 16)
    inverse_col = dot(pair, jnp.where(pick_row == 0, 1.0, 0.0).astype(BF16), TN)
    factor_col = dot(pair, jnp.where(pick_row == 8, 1.0, 0.0).astype(BF16), TN)
    power_ref[...] = inverse_col
    align_ref[...] = factor_col

    def grad_sum(h):
        grad = (power_ref[...] * scaled_grad(h) - align_ref[...] * mixed_ref[h]).astype(BF16)
        grad_ref[h] = grad
        sum_ref[1, h] = dot(squery_ref[h], grad, TN)

    for p in range(2):
        for h in phase(p):
            grad_sum(other + h)
            core_copy(1, h).start()
        if p == 0:
            for h in phase(p):
                grad_sum(own + h)
    send_up(1, 1 - core, 0)
    for h in phase(1):
        grad_sum(own + h)
    send_up(1, 1 - core, 1)

    def inner_grads(h, carry):
        cols = head_cols(h)
        grad = grad_ref[h]
        back = (dot(grad, v_ref[:, cols], NT) * weight_ref[h]).astype(BF16)
        dq = dot(back, k_ref[:, cols], NN) + dot(grad, low_ref[0, h], NT) * qdecay_ref[h]
        dq_ref[:, cols] = dq.astype(BF16)
        dkp_ref[h] = dot(back, q_ref[:, cols], TN)
        dvp_ref[h] = dot(attend_ref[h], grad, TN)
        return carry

    lax.fori_loop(0, heads, inner_grads, 0)

    scan_and_send_down(1, 0)
    scan_and_send_down(1, 1)

    def outer_grads(h):
        cols = head_cols(h)
        decay = kdecay_ref[h]
        low = low_ref[1, h]
        dk_ref[:, cols] = (dkp_ref[h] + dot(v_ref[:, cols], low, NT) * decay).astype(BF16)
        dv_ref[:, cols] = (dvp_ref[h] + dot(k_ref[:, cols], low, NN) * decay).astype(BF16)

    deliver(1, 1 - core, outer_grads)

    log_copy.wait_send()
    sums_all.wait_send()
    rate_all.wait_send()
    for way in range(2):
        part, given = srecv_ref.at[way], give_ref.at[way]
        remote(part, part, cs_sem.at[way], cr_sem.at[way, 0], partner).wait_send()
        remote(given, given, es_sem.at[way], er_sem.at[way, 0], partner).wait_send()
        for sent in sent_all(way):
            sent.wait_send()


def hand_over(dq_ref, dk_ref, dv_ref, dq_out, dk_out, dv_out, sems):
    copies = [
        pltpu.make_async_copy(src, dst, sems.at[n])
        for n, (src, dst) in enumerate([(dq_ref, dq_out), (dk_ref, dk_out), (dv_ref, dv_out)])
    ]
    for copy in copies:
        copy.start()
    for copy in copies:
        copy.wait()


def body(queries, key_rows, value_rows, log_decay, out_grad, norm_gain):
    length, width = queries.shape
    heads = width // DIM
    ny = lax.axis_size("head")
    chips = lax.axis_size("ctx") // 2
    nx = heads // 2
    nz = chips // nx
    half = heads // 2
    rows = DIM // (2 * nz)
    out = jax.ShapeDtypeStruct((length, width), BF16)
    vmem = pl.BlockSpec(memory_space=pltpu.VMEM)
    dma = pltpu.SemaphoreType.DMA
    hbm = pl.BlockSpec(memory_space=pl.ANY)
    inner = pltpu.VMEM((length, width), BF16)
    grads = pl.pallas_call(
        functools.partial(kernel, heads, nx, nz, ny),
        out_shape=(inner, inner, inner),
        in_specs=[hbm] * 6,
        out_specs=(vmem, vmem, vmem),
        scratch_shapes=[
            pltpu.VMEM((length, width), BF16),
            pltpu.VMEM((length, width), BF16),
            pltpu.VMEM((length, width), BF16),
            pltpu.VMEM((heads, BLOCK), F32),
            pltpu.VMEM((length, width), BF16),
            pltpu.VMEM((heads, DIM), F32),
            pltpu.VMEM((heads, BLOCK, DIM), F32),
            pltpu.VMEM((heads, BLOCK), F32),
            pltpu.VMEM((heads, 1, DIM), F32),
            pltpu.VMEM((heads, 1, DIM), F32),
            pltpu.VMEM((half // 2, 2, 1, DIM), F32),
            pltpu.VMEM((chips, 2, 1, DIM), F32),
            pltpu.VMEM((chips, 2, 1, DIM), F32),
            pltpu.VMEM((heads, BLOCK, BLOCK), F32),
            pltpu.VMEM((heads, BLOCK, BLOCK), BF16),
            pltpu.VMEM((heads, BLOCK, DIM), F32),
            pltpu.VMEM((heads, BLOCK, DIM), BF16),
            pltpu.VMEM((heads, BLOCK, DIM), BF16),
            pltpu.VMEM((heads, BLOCK, DIM), F32),
            pltpu.VMEM((heads, BLOCK, DIM), F32),
            pltpu.VMEM((heads, BLOCK, DIM), F32),
            pltpu.VMEM((heads, BLOCK, DIM), F32),
            pltpu.VMEM((BLOCK, DIM), F32),
            pltpu.VMEM((BLOCK, DIM), F32),
            pltpu.VMEM((8, BLOCK), F32),
            pltpu.VMEM((ny, 8, BLOCK), F32),
            pltpu.VMEM((2, heads, DIM, DIM), F32),
            pltpu.VMEM((2, half, DIM, DIM), F32),
            pltpu.VMEM((2, half, DIM, DIM), F32),
            pltpu.VMEM((2, 2, chips, rows, DIM), F32),
            pltpu.VMEM((2, 2, chips, rows, DIM), F32),
            pltpu.VMEM((2, half, DIM, DIM), F32),
            pltpu.VMEM((2, half, DIM, DIM), F32),
            pltpu.VMEM((2, half, DIM, DIM), F32),
            pltpu.VMEM((2, heads, DIM, DIM), BF16),
            dma((6,)),
            dma((2,)),
            dma((2,)),
            dma((1,)),
            dma((1,)),
            dma((2,)),
            dma((2, half)),
            dma((2,)),
            dma((2, 2)),
            dma((2,)),
            dma((2, 2)),
            dma((2,)),
            dma((2, half)),
        ],
        compiler_params=pltpu.CompilerParams(
            collective_id=0, has_side_effects=True, vmem_limit_bytes=60 * 2**20
        ),
        name="lightning",
    )(
        queries, key_rows, value_rows, log_decay, out_grad,
        norm_gain.reshape(heads, DIM),
    )
    return pl.pallas_call(
        hand_over,
        out_shape=(out, out, out),
        in_specs=[vmem] * 3,
        out_specs=(hbm, hbm, hbm),
        scratch_shapes=[dma((3,))],
        name="hand_over",
    )(*(pltpu.with_memory_space_constraint(x, pltpu.VMEM) for x in grads))


def solution(mesh):
    return jax.shard_map(
        body,
        mesh=mesh,
        in_specs=(
            P("ctx", "head"),
            P("ctx", "head"),
            P("ctx", "head"),
            P("head", "ctx"),
            P("ctx", "head"),
            P("head"),
        ),
        out_specs=(P("ctx", "head"), P("ctx", "head"), P("ctx", "head")),
        check_vma=False,
    )
```

```python
import functools

import jax
import jax.numpy as jnp
from jax import lax
from jax.experimental import pallas as pl
from jax.experimental.pallas import tpu as pltpu
from jax.sharding import PartitionSpec as P

DIM = 128
BLOCK = 256
F32 = jnp.float32
BF16 = jnp.bfloat16
HIGH = lax.Precision.HIGHEST
NN = (((1,), (0,)), ((), ()))
NT = (((1,), (1,)), ((), ()))
TN = (((0,), (0,)), ((), ()))


def dot(a, b, dims, precision=None):
    return lax.dot_general(a, b, dims, precision=precision, preferred_element_type=F32)


def ring_order(count):
    return sorted(range(count), key=lambda step: (-min(step, count - step), step))


def split3(x, axis):
    high = x.astype(BF16)
    rest = x - high.astype(F32)
    middle = rest.astype(BF16)
    low = (rest - middle.astype(F32)).astype(BF16)
    return jnp.concatenate([high, middle, low], axis=axis)


def kernel(
    heads, nx, nz, ny,
    q_hbm, k_hbm, v_hbm, ld_hbm, og_hbm, gain_hbm,
    dq_ref, dk_ref, dv_ref,
    q_ref, k_ref, v_ref, ld_ref, og_ref, gain_ref,
    col_ref, cum_ref, end_ref, pend_ref, lrep_ref, lin_ref, rate_ref,
    weight_ref, attend_ref, mixed_ref, grad_ref, squery_ref, dkp_ref, dvp_ref,
    qdecay_ref, kdecay_ref, power_ref, align_ref, red_ref, yin_ref,
    sum_ref, srecv_ref, schip_ref, sin_ref, pout_ref, pin_ref, give_ref, erecv_ref, low_ref,
    in_sem, ls_sem, lr_sem, ys_sem, yr_sem,
    cs_sem, cr_sem, us_sem, ur_sem, ds_sem, dr_sem, es_sem, er_sem,
):
    chips = nx * nz
    own_count = heads // 2
    phase_heads = own_count // 2
    share = nx // phase_heads
    rows = DIM // (share * nz)
    ctx = lax.axis_index("ctx")
    yy = lax.axis_index("head")
    core = lax.rem(ctx, 2)
    chip = lax.div(ctx, 2)
    mx = lax.div(chip, nz)
    mz = lax.rem(chip, nz)
    own = own_count * core
    other = own_count * (1 - core)
    partner = {"ctx": 2 * chip + (1 - core)}
    px = [lax.rem(mx + o, nx) for o in range(nx)]
    pz = [lax.rem(mz + o, nz) for o in range(nz)]
    index_of = [[px[ox] * nz + pz[oz] for oz in range(nz)] for ox in range(nx)]
    offsets = sorted(
        [(ox, oz) for ox in ring_order(nx) for oz in ring_order(nz) if (ox, oz) != (0, 0)],
        key=lambda o: -(min(o[0], nx - o[0]) + min(o[1], nz - o[1])),
    )
    seat = [lax.div(x, share) for x in px]
    lane = [lax.rem(x, share) * nz for x in px]

    def chip_id(index):
        return {"ctx": 2 * index + core}

    def remote(src, dst, send, recv, device):
        return pltpu.make_async_remote_copy(
            src_ref=src, dst_ref=dst, send_sem=send, recv_sem=recv,
            device_id=device, device_id_type=pl.DeviceIdType.MESH,
        )

    barrier = pltpu.get_barrier_semaphore()

    def greet(device):
        pl.semaphore_signal(
            barrier, inc=1, device_id=device, device_id_type=pl.DeviceIdType.MESH
        )

    for ox, oz in offsets:
        greet(chip_id(index_of[ox][oz]))
    greet(partner)
    for oy in range(1, ny):
        greet({"head": lax.rem(yy + oy, ny)})

    loads = [
        pltpu.make_async_copy(src, dst, in_sem.at[n])
        for n, (src, dst) in enumerate(
            [
                (ld_hbm, ld_ref), (k_hbm, k_ref), (v_hbm, v_ref),
                (q_hbm, q_ref), (og_hbm, og_ref), (gain_hbm, gain_ref),
            ]
        )
    ]
    for load in loads:
        load.start()

    def head_cols(h):
        return pl.ds(pl.multiple_of(h * DIM, DIM), DIM)

    step_u = lax.broadcasted_iota(jnp.int32, (BLOCK, BLOCK), 0)
    step_t = lax.broadcasted_iota(jnp.int32, (BLOCK, BLOCK), 1)
    loads[0].wait()
    cum = dot(ld_ref[...], (step_u <= step_t).astype(F32), NN, HIGH)
    cum_ref[...] = cum
    pick = lax.broadcasted_iota(jnp.int32, (heads, DIM), 0)
    for h in range(heads):
        col = dot(cum, (pick == h).astype(F32), TN, HIGH)
        col_ref[h] = col
        end_ref[h] = col[BLOCK - 1 : BLOCK, :]
    loads[1].wait()
    loads[2].wait()

    def key_sum(i, base):
        h = base + i
        decay = jnp.exp(end_ref[h] - col_ref[h])
        kdecay_ref[h] = decay
        keyed = (k_ref[:, head_cols(h)].astype(F32) * decay).astype(BF16)
        sum_ref[0, h] = dot(keyed, v_ref[:, head_cols(h)], TN)
        return base

    def core_copy(way, i):
        return remote(
            sum_ref.at[way, other + i], srecv_ref.at[way, i],
            cs_sem.at[way], cr_sem.at[way, i], partner,
        )

    log_copy = remote(end_ref, pend_ref, ls_sem.at[1], lr_sem.at[1], partner)

    lax.fori_loop(0, own_count, key_sum, other)
    lax.fori_loop(0, own_count, key_sum, own)
    loads[3].wait()

    pl.semaphore_wait(barrier, chips - 1 + 1 + ny - 1)

    log_copy.start()
    for h in range(own_count):
        core_copy(0, h).start()

    log_copy.wait_recv()
    for p in range(2):
        for j in range(phase_heads):
            i = own + phase_heads * p + j
            lrep_ref[j, p] = end_ref[i] + pend_ref[i]

    def rate_copy(ox, oz):
        index = index_of[ox][oz]
        return remote(
            lrep_ref.at[seat[ox]], lin_ref.at[chip], ls_sem.at[0], lr_sem.at[0],
            chip_id(index),
        )

    lin_most = lin_ref.at[pl.ds(0, chips - 1)]
    rate_all = remote(lin_most, lin_most, ls_sem.at[0], lr_sem.at[0], partner)

    def slice_of(ox, oz):
        return pl.ds(pl.multiple_of((lane[ox] + pz[oz]) * rows, rows), rows)

    def up_copy(way, p, ox, oz):
        index = index_of[ox][oz]
        return remote(
            schip_ref.at[way, phase_heads * p + seat[ox], slice_of(ox, oz)],
            sin_ref.at[way, p, chip],
            us_sem.at[way], ur_sem.at[way, p], chip_id(index),
        )

    def up_all(way, p):
        most = sin_ref.at[way, p, pl.ds(0, chips - 1)]
        return remote(most, most, us_sem.at[way], ur_sem.at[way, p], partner)

    def down_copy(way, p, ox, oz):
        index = index_of[ox][oz]
        return remote(
            pout_ref.at[way, p, index],
            pin_ref.at[way, phase_heads * p + seat[0], slice_of(0, 0)],
            ds_sem.at[way], dr_sem.at[way, p], chip_id(index),
        )

    def down_all(way, p):
        most = pout_ref.at[way, p, pl.ds(0, chips - 1)]
        return remote(most, most, ds_sem.at[way], dr_sem.at[way, p], partner)

    def sent_all(way):
        up = sin_ref.at[way, pl.ds(0, 2), pl.ds(0, chips - 1)]
        down = pout_ref.at[way, pl.ds(0, 2), pl.ds(0, chips - 1)]
        return (
            remote(up, up, us_sem.at[way], ur_sem.at[way, 0], partner),
            remote(down, down, ds_sem.at[way], dr_sem.at[way, 0], partner),
        )

    def give_copy(way, h):
        return remote(
            give_ref.at[way, h], erecv_ref.at[way, h],
            es_sem.at[way], er_sem.at[way, h], partner,
        )

    one = jnp.ones((1, DIM), F32)
    none = jnp.zeros((1, DIM), F32)

    def phase(p):
        return range(phase_heads * p, phase_heads * (p + 1))

    def send_up(way, cc, p):
        for h in phase(p):
            core_copy(way, h).wait_recv()
            mine = jnp.where(cc == 0, jnp.exp(pend_ref[own + h]), one)
            theirs = jnp.where(cc == 0, one, jnp.exp(end_ref[own + h]))
            schip_ref[way, h] = mine * sum_ref[way, own + h] + theirs * srecv_ref[way, h]
        for ox, oz in offsets:
            up_copy(way, p, ox, oz).start()
        sin_ref[way, p, chip] = schip_ref[way, phase_heads * p + seat[0], slice_of(0, 0), :]

    def scan_and_send_down(way, p):
        up_all(way, p).wait_recv()

        def advance(step, carry):
            index = step if way == 0 else chips - 1 - step
            pout_ref[way, p, index] = carry
            return rate_ref[index, p] * carry + sin_ref[way, p, index]

        lax.fori_loop(0, chips, advance, jnp.zeros((rows, DIM), F32), unroll=8)
        for ox, oz in offsets:
            down_copy(way, p, ox, oz).start()
        pin_ref[way, phase_heads * p + seat[0], slice_of(0, 0), :] = pout_ref[way, p, chip]

    def take_own(way, cc, h):
        before = pin_ref[way, h]
        give_ref[way, h] = (
            jnp.where(cc == 0, jnp.exp(end_ref[own + h]), one) * before
            + jnp.where(cc == 0, one, none) * sum_ref[way, own + h]
        )
        give_copy(way, h).start()
        low_ref[way, own + h] = (
            jnp.where(cc == 0, one, jnp.exp(pend_ref[own + h])) * before
            + jnp.where(cc == 0, none, one) * srecv_ref[way, h]
        ).astype(BF16)

    def take_other(way, h):
        give_copy(way, h).wait_recv()
        low_ref[way, other + h] = erecv_ref[way, h].astype(BF16)

    def deliver(way, cc, use):
        for p in range(2):
            down_all(way, p).wait_recv()
            for h in phase(p):
                take_own(way, cc, h)
            for h in phase(p):
                use(own + h)
            for h in phase(p):
                take_other(way, h)
                use(other + h)

    for ox, oz in offsets:
        rate_copy(ox, oz).start()
    lin_ref[chip] = lrep_ref[seat[0]]
    send_up(0, core, 0)
    send_up(0, core, 1)

    lower = step_t <= step_u

    def inner_out(h, carry):
        col = col_ref[h]
        gap = jnp.concatenate([col, col], axis=1) - cum_ref[pl.ds(h, 1), :]
        weight = jnp.where(lower, jnp.exp(jnp.where(lower, gap, 0.0)), 0.0)
        weight_ref[h] = weight
        q = q_ref[:, head_cols(h)]
        attend = (dot(q, k_ref[:, head_cols(h)], NT) * weight).astype(BF16)
        attend_ref[h] = attend
        mixed_ref[h] = dot(attend, v_ref[:, head_cols(h)], NN)
        decay = jnp.exp(col)
        qdecay_ref[h] = decay
        squery_ref[h] = (q.astype(F32) * decay).astype(BF16)
        return carry

    lax.fori_loop(0, heads, inner_out, 0)
    loads[4].wait()
    loads[5].wait()
    power_ref[...] = jnp.zeros_like(power_ref)
    align_ref[...] = jnp.zeros_like(align_ref)

    rate_all.wait_recv()
    rate_ref[...] = jnp.exp(lin_ref[...])

    scan_and_send_down(0, 0)
    scan_and_send_down(0, 1)

    def scaled_grad(h):
        return og_ref[:, head_cols(h)].astype(F32) * gain_ref[pl.ds(h, 1), :]

    def outer_out(h):
        mixed = mixed_ref[h] + dot(q_ref[:, head_cols(h)], low_ref[0, h], NN) * qdecay_ref[h]
        mixed_ref[h] = mixed
        power_ref[...] += mixed * mixed
        align_ref[...] += scaled_grad(h) * mixed

    deliver(0, core, outer_out)

    ones = jnp.ones((8, 3 * DIM), BF16)
    sums_row = lax.broadcasted_iota(jnp.int32, (8, BLOCK), 0)
    red_ref[...] = jnp.where(
        sums_row < 4,
        dot(ones, split3(power_ref[...], 1), NT),
        dot(ones, split3(align_ref[...], 1), NT),
    )

    def sums_copy(oy):
        to = lax.rem(yy + oy, ny)
        return remote(red_ref, yin_ref.at[yy], ys_sem.at[0], yr_sem.at[0], {"head": to})

    yin_most = yin_ref.at[pl.ds(0, ny - 1)]
    sums_all = remote(yin_most, yin_most, ys_sem.at[0], yr_sem.at[0], partner)

    for oy in range(1, ny):
        sums_copy(oy).start()
    yin_ref[yy] = red_ref[...]
    sums_all.wait_recv()
    total = yin_ref[0]
    for index in range(1, ny):
        total = total + yin_ref[index]
    features = heads * DIM * ny
    inverse = lax.rsqrt(total[0:1, :] / features + 1e-6)
    factor = inverse * inverse * inverse * (total[4:5, :] / features)
    pair_row = lax.broadcasted_iota(jnp.int32, (16, BLOCK), 0)
    pair = split3(jnp.where(pair_row < 8, inverse, factor), 0)
    pick_row = lax.rem(lax.broadcasted_iota(jnp.int32, (48, DIM), 0), 16)
    inverse_col = dot(pair, jnp.where(pick_row == 0, 1.0, 0.0).astype(BF16), TN)
    factor_col = dot(pair, jnp.where(pick_row == 8, 1.0, 0.0).astype(BF16), TN)
    power_ref[...] = inverse_col
    align_ref[...] = factor_col

    def grad_sum(h):
        grad = (power_ref[...] * scaled_grad(h) - align_ref[...] * mixed_ref[h]).astype(BF16)
        grad_ref[h] = grad
        sum_ref[1, h] = dot(squery_ref[h], grad, TN)

    for p in range(2):
        for h in phase(p):
            grad_sum(other + h)
            core_copy(1, h).start()
        if p == 0:
            for h in phase(p):
                grad_sum(own + h)
    send_up(1, 1 - core, 0)
    for h in phase(1):
        grad_sum(own + h)
    send_up(1, 1 - core, 1)

    def inner_grads(h, carry):
        cols = head_cols(h)
        grad = grad_ref[h]
        back = (dot(grad, v_ref[:, cols], NT) * weight_ref[h]).astype(BF16)
        dq = dot(back, k_ref[:, cols], NN) + dot(grad, low_ref[0, h], NT) * qdecay_ref[h]
        dq_ref[:, cols] = dq.astype(BF16)
        dkp_ref[h] = dot(back, q_ref[:, cols], TN)
        dvp_ref[h] = dot(attend_ref[h], grad, TN)
        return carry

    lax.fori_loop(0, heads, inner_grads, 0)

    scan_and_send_down(1, 0)
    scan_and_send_down(1, 1)

    def outer_grads(h):
        cols = head_cols(h)
        decay = kdecay_ref[h]
        low = low_ref[1, h]
        dk_ref[:, cols] = (dkp_ref[h] + dot(v_ref[:, cols], low, NT) * decay).astype(BF16)
        dv_ref[:, cols] = (dvp_ref[h] + dot(k_ref[:, cols], low, NN) * decay).astype(BF16)

    deliver(1, 1 - core, outer_grads)

    log_copy.wait_send()
    sums_all.wait_send()
    rate_all.wait_send()
    for way in range(2):
        part, given = srecv_ref.at[way], give_ref.at[way]
        remote(part, part, cs_sem.at[way], cr_sem.at[way, 0], partner).wait_send()
        remote(given, given, es_sem.at[way], er_sem.at[way, 0], partner).wait_send()
        for sent in sent_all(way):
            sent.wait_send()


def hand_over(dq_ref, dk_ref, dv_ref, dq_out, dk_out, dv_out, sems):
    copies = [
        pltpu.make_async_copy(src, dst, sems.at[n])
        for n, (src, dst) in enumerate([(dq_ref, dq_out), (dk_ref, dk_out), (dv_ref, dv_out)])
    ]
    for copy in copies:
        copy.start()
    for copy in copies:
        copy.wait()


def body(queries, key_rows, value_rows, log_decay, out_grad, norm_gain):
    length, width = queries.shape
    heads = width // DIM
    ny = lax.axis_size("head")
    chips = lax.axis_size("ctx") // 2
    nx = heads // 2
    nz = chips // nx
    half = heads // 2
    rows = DIM // (2 * nz)
    out = jax.ShapeDtypeStruct((length, width), BF16)
    vmem = pl.BlockSpec(memory_space=pltpu.VMEM)
    dma = pltpu.SemaphoreType.DMA
    hbm = pl.BlockSpec(memory_space=pl.ANY)
    inner = pltpu.VMEM((length, width), BF16)
    grads = pl.pallas_call(
        functools.partial(kernel, heads, nx, nz, ny),
        out_shape=(inner, inner, inner),
        in_specs=[hbm] * 6,
        out_specs=(vmem, vmem, vmem),
        scratch_shapes=[
            pltpu.VMEM((length, width), BF16),
            pltpu.VMEM((length, width), BF16),
            pltpu.VMEM((length, width), BF16),
            pltpu.VMEM((heads, BLOCK), F32),
            pltpu.VMEM((length, width), BF16),
            pltpu.VMEM((heads, DIM), F32),
            pltpu.VMEM((heads, BLOCK, DIM), F32),
            pltpu.VMEM((heads, BLOCK), F32),
            pltpu.VMEM((heads, 1, DIM), F32),
            pltpu.VMEM((heads, 1, DIM), F32),
            pltpu.VMEM((half // 2, 2, 1, DIM), F32),
            pltpu.VMEM((chips, 2, 1, DIM), F32),
            pltpu.VMEM((chips, 2, 1, DIM), F32),
            pltpu.VMEM((heads, BLOCK, BLOCK), F32),
            pltpu.VMEM((heads, BLOCK, BLOCK), BF16),
            pltpu.VMEM((heads, BLOCK, DIM), F32),
            pltpu.VMEM((heads, BLOCK, DIM), BF16),
            pltpu.VMEM((heads, BLOCK, DIM), BF16),
            pltpu.VMEM((heads, BLOCK, DIM), F32),
            pltpu.VMEM((heads, BLOCK, DIM), F32),
            pltpu.VMEM((heads, BLOCK, DIM), F32),
            pltpu.VMEM((heads, BLOCK, DIM), F32),
            pltpu.VMEM((BLOCK, DIM), F32),
            pltpu.VMEM((BLOCK, DIM), F32),
            pltpu.VMEM((8, BLOCK), F32),
            pltpu.VMEM((ny, 8, BLOCK), F32),
            pltpu.VMEM((2, heads, DIM, DIM), F32),
            pltpu.VMEM((2, half, DIM, DIM), F32),
            pltpu.VMEM((2, half, DIM, DIM), F32),
            pltpu.VMEM((2, 2, chips, rows, DIM), F32),
            pltpu.VMEM((2, 2, chips, rows, DIM), F32),
            pltpu.VMEM((2, half, DIM, DIM), F32),
            pltpu.VMEM((2, half, DIM, DIM), F32),
            pltpu.VMEM((2, half, DIM, DIM), F32),
            pltpu.VMEM((2, heads, DIM, DIM), BF16),
            dma((6,)),
            dma((2,)),
            dma((2,)),
            dma((1,)),
            dma((1,)),
            dma((2,)),
            dma((2, half)),
            dma((2,)),
            dma((2, 2)),
            dma((2,)),
            dma((2, 2)),
            dma((2,)),
            dma((2, half)),
        ],
        compiler_params=pltpu.CompilerParams(
            collective_id=0, has_side_effects=True, vmem_limit_bytes=60 * 2**20
        ),
        name="lightning",
    )(
        queries, key_rows, value_rows, log_decay, out_grad,
        norm_gain.reshape(heads, DIM),
    )
    return pl.pallas_call(
        hand_over,
        out_shape=(out, out, out),
        in_specs=[vmem] * 3,
        out_specs=(hbm, hbm, hbm),
        scratch_shapes=[dma((3,))],
        name="hand_over",
    )(*(pltpu.with_memory_space_constraint(x, pltpu.VMEM) for x in grads))


def solution(mesh):
    return jax.shard_map(
        body,
        mesh=mesh,
        in_specs=(
            P("ctx", "head"),
            P("ctx", "head"),
            P("ctx", "head"),
            P("head", "ctx"),
            P("ctx", "head"),
            P("head"),
        ),
        out_specs=(P("ctx", "head"), P("ctx", "head"), P("ctx", "head")),
        check_vma=False,
    )
```

```python
import functools

import jax
import jax.numpy as jnp
from jax import lax
from jax.experimental import pallas as pl
from jax.experimental.pallas import tpu as pltpu
from jax.sharding import PartitionSpec as P

DIM = 128
BLOCK = 256
F32 = jnp.float32
BF16 = jnp.bfloat16
HIGH = lax.Precision.HIGHEST
NN = (((1,), (0,)), ((), ()))
NT = (((1,), (1,)), ((), ()))
TN = (((0,), (0,)), ((), ()))


def dot(a, b, dims, precision=None):
    return lax.dot_general(a, b, dims, precision=precision, preferred_element_type=F32)


def ring_order(count):
    return sorted(range(count), key=lambda step: (-min(step, count - step), step))


def split3(x, axis):
    high = x.astype(BF16)
    rest = x - high.astype(F32)
    middle = rest.astype(BF16)
    low = (rest - middle.astype(F32)).astype(BF16)
    return jnp.concatenate([high, middle, low], axis=axis)


def kernel(
    heads, nx, nz, ny,
    q_hbm, k_hbm, v_hbm, ld_hbm, og_hbm, gain_hbm,
    dq_ref, dk_ref, dv_ref,
    q_ref, k_ref, v_ref, ld_ref, og_ref, gain_ref,
    col_ref, cum_ref, end_ref, pend_ref, lrep_ref, lin_ref, rate_ref,
    weight_ref, attend_ref, mixed_ref, grad_ref, squery_ref, dkp_ref, dvp_ref,
    qdecay_ref, kdecay_ref, power_ref, align_ref, red_ref, yin_ref,
    sum_ref, srecv_ref, schip_ref, sin_ref, pout_ref, pin_ref, give_ref, erecv_ref, low_ref,
    in_sem, ls_sem, lr_sem, ys_sem, yr_sem,
    cs_sem, cr_sem, us_sem, ur_sem, ds_sem, dr_sem, es_sem, er_sem,
):
    chips = nx * nz
    own_count = heads // 2
    phase_heads = own_count // 2
    share = nx // phase_heads
    rows = DIM // (share * nz)
    ctx = lax.axis_index("ctx")
    yy = lax.axis_index("head")
    core = lax.rem(ctx, 2)
    chip = lax.div(ctx, 2)
    mx = lax.div(chip, nz)
    mz = lax.rem(chip, nz)
    own = own_count * core
    other = own_count * (1 - core)
    partner = {"ctx": 2 * chip + (1 - core)}
    px = [lax.rem(mx + o, nx) for o in range(nx)]
    pz = [lax.rem(mz + o, nz) for o in range(nz)]
    index_of = [[px[ox] * nz + pz[oz] for oz in range(nz)] for ox in range(nx)]
    offsets = sorted(
        [(ox, oz) for ox in ring_order(nx) for oz in ring_order(nz) if (ox, oz) != (0, 0)],
        key=lambda o: -(min(o[0], nx - o[0]) + min(o[1], nz - o[1])),
    )
    seat = [lax.div(x, share) for x in px]
    lane = [lax.rem(x, share) * nz for x in px]

    def chip_id(index):
        return {"ctx": 2 * index + core}

    def remote(src, dst, send, recv, device):
        return pltpu.make_async_remote_copy(
            src_ref=src, dst_ref=dst, send_sem=send, recv_sem=recv,
            device_id=device, device_id_type=pl.DeviceIdType.MESH,
        )

    barrier = pltpu.get_barrier_semaphore()

    def greet(device):
        pl.semaphore_signal(
            barrier, inc=1, device_id=device, device_id_type=pl.DeviceIdType.MESH
        )

    for ox, oz in offsets:
        greet(chip_id(index_of[ox][oz]))
    greet(partner)
    for oy in range(1, ny):
        greet({"head": lax.rem(yy + oy, ny)})

    loads = [
        pltpu.make_async_copy(src, dst, in_sem.at[n])
        for n, (src, dst) in enumerate(
            [
                (ld_hbm, ld_ref), (k_hbm, k_ref), (v_hbm, v_ref),
                (q_hbm, q_ref), (og_hbm, og_ref), (gain_hbm, gain_ref),
            ]
        )
    ]
    for load in loads:
        load.start()

    def head_cols(h):
        return pl.ds(pl.multiple_of(h * DIM, DIM), DIM)

    step_u = lax.broadcasted_iota(jnp.int32, (BLOCK, BLOCK), 0)
    step_t = lax.broadcasted_iota(jnp.int32, (BLOCK, BLOCK), 1)
    loads[0].wait()
    cum = dot(ld_ref[...], (step_u <= step_t).astype(F32), NN, HIGH)
    cum_ref[...] = cum
    pick = lax.broadcasted_iota(jnp.int32, (heads, DIM), 0)
    for h in range(heads):
        col = dot(cum, (pick == h).astype(F32), TN, HIGH)
        col_ref[h] = col
        end_ref[h] = col[BLOCK - 1 : BLOCK, :]
    loads[1].wait()
    loads[2].wait()

    def key_sum(i, base):
        h = base + i
        decay = jnp.exp(end_ref[h] - col_ref[h])
        kdecay_ref[h] = decay
        keyed = (k_ref[:, head_cols(h)].astype(F32) * decay).astype(BF16)
        sum_ref[0, h] = dot(keyed, v_ref[:, head_cols(h)], TN)
        return base

    def core_copy(way, i):
        return remote(
            sum_ref.at[way, other + i], srecv_ref.at[way, i],
            cs_sem.at[way], cr_sem.at[way, (i // phase_heads)], partner,
        )

    log_copy = remote(end_ref, pend_ref, ls_sem.at[1], lr_sem.at[1], partner)

    lax.fori_loop(0, own_count, key_sum, other)
    lax.fori_loop(0, own_count, key_sum, own)
    loads[3].wait()

    pl.semaphore_wait(barrier, chips - 1 + 1 + ny - 1)

    log_copy.start()
    for h in range(own_count):
        core_copy(0, h).start()

    log_copy.wait_recv()
    for p in range(2):
        for j in range(phase_heads):
            i = own + phase_heads * p + j
            lrep_ref[j, p] = end_ref[i] + pend_ref[i]

    def rate_copy(ox, oz):
        index = index_of[ox][oz]
        return remote(
            lrep_ref.at[seat[ox]], lin_ref.at[chip], ls_sem.at[0], lr_sem.at[0],
            chip_id(index),
        )

    lin_most = lin_ref.at[pl.ds(0, chips - 1)]
    rate_all = remote(lin_most, lin_most, ls_sem.at[0], lr_sem.at[0], partner)

    def slice_of(ox, oz):
        return pl.ds(pl.multiple_of((lane[ox] + pz[oz]) * rows, rows), rows)

    def up_copy(way, p, ox, oz):
        index = index_of[ox][oz]
        return remote(
            schip_ref.at[way, phase_heads * p + seat[ox], slice_of(ox, oz)],
            sin_ref.at[way, p, chip],
            us_sem.at[way], ur_sem.at[way, p], chip_id(index),
        )

    def up_all(way, p):
        most = sin_ref.at[way, p, pl.ds(0, chips - 1)]
        return remote(most, most, us_sem.at[way], ur_sem.at[way, p], partner)

    def down_copy(way, p, ox, oz):
        index = index_of[ox][oz]
        return remote(
            pout_ref.at[way, p, index],
            pin_ref.at[way, phase_heads * p + seat[0], slice_of(0, 0)],
            ds_sem.at[way], dr_sem.at[way, p], chip_id(index),
        )

    def down_all(way, p):
        most = pout_ref.at[way, p, pl.ds(0, chips - 1)]
        return remote(most, most, ds_sem.at[way], dr_sem.at[way, p], partner)

    def sent_all(way):
        up = sin_ref.at[way, pl.ds(0, 2), pl.ds(0, chips - 1)]
        down = pout_ref.at[way, pl.ds(0, 2), pl.ds(0, chips - 1)]
        return (
            remote(up, up, us_sem.at[way], ur_sem.at[way, 0], partner),
            remote(down, down, ds_sem.at[way], dr_sem.at[way, 0], partner),
        )

    def give_copy(way, h):
        return remote(
            give_ref.at[way, h], erecv_ref.at[way, h],
            es_sem.at[way], er_sem.at[way, h], partner,
        )

    one = jnp.ones((1, DIM), F32)
    none = jnp.zeros((1, DIM), F32)

    def phase(p):
        return range(phase_heads * p, phase_heads * (p + 1))

    def send_up(way, cc, p):
        part = srecv_ref.at[way, pl.ds(phase_heads * p, phase_heads)]
        remote(part, part, cs_sem.at[way], cr_sem.at[way, p], partner).wait_recv()
        for h in phase(p):
            mine = jnp.where(cc == 0, jnp.exp(pend_ref[own + h]), one)
            theirs = jnp.where(cc == 0, one, jnp.exp(end_ref[own + h]))
            schip_ref[way, h] = mine * sum_ref[way, own + h] + theirs * srecv_ref[way, h]
        for ox, oz in offsets:
            up_copy(way, p, ox, oz).start()
        sin_ref[way, p, chip] = schip_ref[way, phase_heads * p + seat[0], slice_of(0, 0), :]

    def scan_and_send_down(way, p):
        up_all(way, p).wait_recv()

        def advance(step, carry):
            index = step if way == 0 else chips - 1 - step
            pout_ref[way, p, index] = carry
            return rate_ref[index, p] * carry + sin_ref[way, p, index]

        lax.fori_loop(0, chips, advance, jnp.zeros((rows, DIM), F32), unroll=8)
        for ox, oz in offsets:
            down_copy(way, p, ox, oz).start()
        pin_ref[way, phase_heads * p + seat[0], slice_of(0, 0), :] = pout_ref[way, p, chip]

    def take_own(way, cc, h):
        before = pin_ref[way, h]
        give_ref[way, h] = (
            jnp.where(cc == 0, jnp.exp(end_ref[own + h]), one) * before
            + jnp.where(cc == 0, one, none) * sum_ref[way, own + h]
        )
        give_copy(way, h).start()
        low_ref[way, own + h] = (
            jnp.where(cc == 0, one, jnp.exp(pend_ref[own + h])) * before
            + jnp.where(cc == 0, none, one) * srecv_ref[way, h]
        ).astype(BF16)

    def take_other(way, h):
        give_copy(way, h).wait_recv()
        low_ref[way, other + h] = erecv_ref[way, h].astype(BF16)

    def deliver(way, cc, use):
        for p in range(2):
            down_all(way, p).wait_recv()
            for h in phase(p):
                take_own(way, cc, h)
            for h in phase(p):
                use(own + h)
            for h in phase(p):
                take_other(way, h)
                use(other + h)

    for ox, oz in offsets:
        rate_copy(ox, oz).start()
    lin_ref[chip] = lrep_ref[seat[0]]
    send_up(0, core, 0)
    send_up(0, core, 1)

    lower = step_t <= step_u

    def inner_out(h, carry):
        col = col_ref[h]
        gap = jnp.concatenate([col, col], axis=1) - cum_ref[pl.ds(h, 1), :]
        weight = jnp.where(lower, jnp.exp(jnp.where(lower, gap, 0.0)), 0.0)
        weight_ref[h] = weight
        q = q_ref[:, head_cols(h)]
        attend = (dot(q, k_ref[:, head_cols(h)], NT) * weight).astype(BF16)
        attend_ref[h] = attend
        mixed_ref[h] = dot(attend, v_ref[:, head_cols(h)], NN)
        decay = jnp.exp(col)
        qdecay_ref[h] = decay
        squery_ref[h] = (q.astype(F32) * decay).astype(BF16)
        return carry

    lax.fori_loop(0, heads, inner_out, 0)
    loads[4].wait()
    loads[5].wait()
    power_ref[...] = jnp.zeros_like(power_ref)
    align_ref[...] = jnp.zeros_like(align_ref)

    rate_all.wait_recv()
    rate_ref[...] = jnp.exp(lin_ref[...])

    scan_and_send_down(0, 0)
    scan_and_send_down(0, 1)

    def scaled_grad(h):
        return og_ref[:, head_cols(h)].astype(F32) * gain_ref[pl.ds(h, 1), :]

    def outer_out(h):
        mixed = mixed_ref[h] + dot(q_ref[:, head_cols(h)], low_ref[0, h], NN) * qdecay_ref[h]
        mixed_ref[h] = mixed
        power_ref[...] += mixed * mixed
        align_ref[...] += scaled_grad(h) * mixed

    deliver(0, core, outer_out)

    ones = jnp.ones((8, 3 * DIM), BF16)
    sums_row = lax.broadcasted_iota(jnp.int32, (8, BLOCK), 0)
    red_ref[...] = jnp.where(
        sums_row < 4,
        dot(ones, split3(power_ref[...], 1), NT),
        dot(ones, split3(align_ref[...], 1), NT),
    )

    def sums_copy(oy):
        to = lax.rem(yy + oy, ny)
        return remote(red_ref, yin_ref.at[yy], ys_sem.at[0], yr_sem.at[0], {"head": to})

    yin_most = yin_ref.at[pl.ds(0, ny - 1)]
    sums_all = remote(yin_most, yin_most, ys_sem.at[0], yr_sem.at[0], partner)

    for oy in range(1, ny):
        sums_copy(oy).start()
    yin_ref[yy] = red_ref[...]
    sums_all.wait_recv()
    total = yin_ref[0]
    for index in range(1, ny):
        total = total + yin_ref[index]
    features = heads * DIM * ny
    inverse = lax.rsqrt(total[0:1, :] / features + 1e-6)
    factor = inverse * inverse * inverse * (total[4:5, :] / features)
    pair_row = lax.broadcasted_iota(jnp.int32, (16, BLOCK), 0)
    pair = split3(jnp.where(pair_row < 8, inverse, factor), 0)
    pick_row = lax.rem(lax.broadcasted_iota(jnp.int32, (48, DIM), 0), 16)
    inverse_col = dot(pair, jnp.where(pick_row == 0, 1.0, 0.0).astype(BF16), TN)
    factor_col = dot(pair, jnp.where(pick_row == 8, 1.0, 0.0).astype(BF16), TN)
    power_ref[...] = inverse_col
    align_ref[...] = factor_col

    def grad_sum(h):
        grad = (power_ref[...] * scaled_grad(h) - align_ref[...] * mixed_ref[h]).astype(BF16)
        grad_ref[h] = grad
        sum_ref[1, h] = dot(squery_ref[h], grad, TN)

    for p in range(2):
        for h in phase(p):
            grad_sum(other + h)
            core_copy(1, h).start()
        if p == 0:
            for h in phase(p):
                grad_sum(own + h)
    send_up(1, 1 - core, 0)
    for h in phase(1):
        grad_sum(own + h)
    send_up(1, 1 - core, 1)

    def inner_grads(h, carry):
        cols = head_cols(h)
        grad = grad_ref[h]
        back = (dot(grad, v_ref[:, cols], NT) * weight_ref[h]).astype(BF16)
        dq = dot(back, k_ref[:, cols], NN) + dot(grad, low_ref[0, h], NT) * qdecay_ref[h]
        dq_ref[:, cols] = dq.astype(BF16)
        dkp_ref[h] = dot(back, q_ref[:, cols], TN)
        dvp_ref[h] = dot(attend_ref[h], grad, TN)
        return carry

    lax.fori_loop(0, heads, inner_grads, 0)

    scan_and_send_down(1, 0)
    scan_and_send_down(1, 1)

    def outer_grads(h):
        cols = head_cols(h)
        decay = kdecay_ref[h]
        low = low_ref[1, h]
        dk_ref[:, cols] = (dkp_ref[h] + dot(v_ref[:, cols], low, NT) * decay).astype(BF16)
        dv_ref[:, cols] = (dvp_ref[h] + dot(k_ref[:, cols], low, NN) * decay).astype(BF16)

    deliver(1, 1 - core, outer_grads)

    log_copy.wait_send()
    sums_all.wait_send()
    rate_all.wait_send()
    for way in range(2):
        part, given = srecv_ref.at[way], give_ref.at[way]
        remote(part, part, cs_sem.at[way], cr_sem.at[way, 0], partner).wait_send()
        remote(given, given, es_sem.at[way], er_sem.at[way, 0], partner).wait_send()
        for sent in sent_all(way):
            sent.wait_send()


def hand_over(dq_ref, dk_ref, dv_ref, dq_out, dk_out, dv_out, sems):
    copies = [
        pltpu.make_async_copy(src, dst, sems.at[n])
        for n, (src, dst) in enumerate([(dq_ref, dq_out), (dk_ref, dk_out), (dv_ref, dv_out)])
    ]
    for copy in copies:
        copy.start()
    for copy in copies:
        copy.wait()


def body(queries, key_rows, value_rows, log_decay, out_grad, norm_gain):
    length, width = queries.shape
    heads = width // DIM
    ny = lax.axis_size("head")
    chips = lax.axis_size("ctx") // 2
    nx = heads // 2
    nz = chips // nx
    half = heads // 2
    rows = DIM // (2 * nz)
    out = jax.ShapeDtypeStruct((length, width), BF16)
    vmem = pl.BlockSpec(memory_space=pltpu.VMEM)
    dma = pltpu.SemaphoreType.DMA
    hbm = pl.BlockSpec(memory_space=pl.ANY)
    inner = pltpu.VMEM((length, width), BF16)
    grads = pl.pallas_call(
        functools.partial(kernel, heads, nx, nz, ny),
        out_shape=(inner, inner, inner),
        in_specs=[hbm] * 6,
        out_specs=(vmem, vmem, vmem),
        scratch_shapes=[
            pltpu.VMEM((length, width), BF16),
            pltpu.VMEM((length, width), BF16),
            pltpu.VMEM((length, width), BF16),
            pltpu.VMEM((heads, BLOCK), F32),
            pltpu.VMEM((length, width), BF16),
            pltpu.VMEM((heads, DIM), F32),
            pltpu.VMEM((heads, BLOCK, DIM), F32),
            pltpu.VMEM((heads, BLOCK), F32),
            pltpu.VMEM((heads, 1, DIM), F32),
            pltpu.VMEM((heads, 1, DIM), F32),
            pltpu.VMEM((half // 2, 2, 1, DIM), F32),
            pltpu.VMEM((chips, 2, 1, DIM), F32),
            pltpu.VMEM((chips, 2, 1, DIM), F32),
            pltpu.VMEM((heads, BLOCK, BLOCK), F32),
            pltpu.VMEM((heads, BLOCK, BLOCK), BF16),
            pltpu.VMEM((heads, BLOCK, DIM), F32),
            pltpu.VMEM((heads, BLOCK, DIM), BF16),
            pltpu.VMEM((heads, BLOCK, DIM), BF16),
            pltpu.VMEM((heads, BLOCK, DIM), F32),
            pltpu.VMEM((heads, BLOCK, DIM), F32),
            pltpu.VMEM((heads, BLOCK, DIM), F32),
            pltpu.VMEM((heads, BLOCK, DIM), F32),
            pltpu.VMEM((BLOCK, DIM), F32),
            pltpu.VMEM((BLOCK, DIM), F32),
            pltpu.VMEM((8, BLOCK), F32),
            pltpu.VMEM((ny, 8, BLOCK), F32),
            pltpu.VMEM((2, heads, DIM, DIM), F32),
            pltpu.VMEM((2, half, DIM, DIM), F32),
            pltpu.VMEM((2, half, DIM, DIM), F32),
            pltpu.VMEM((2, 2, chips, rows, DIM), F32),
            pltpu.VMEM((2, 2, chips, rows, DIM), F32),
            pltpu.VMEM((2, half, DIM, DIM), F32),
            pltpu.VMEM((2, half, DIM, DIM), F32),
            pltpu.VMEM((2, half, DIM, DIM), F32),
            pltpu.VMEM((2, heads, DIM, DIM), BF16),
            dma((6,)),
            dma((2,)),
            dma((2,)),
            dma((1,)),
            dma((1,)),
            dma((2,)),
            dma((2, 2)),
            dma((2,)),
            dma((2, 2)),
            dma((2,)),
            dma((2, 2)),
            dma((2,)),
            dma((2, half)),
        ],
        compiler_params=pltpu.CompilerParams(
            collective_id=0, has_side_effects=True, vmem_limit_bytes=60 * 2**20
        ),
        name="lightning",
    )(
        queries, key_rows, value_rows, log_decay, out_grad,
        norm_gain.reshape(heads, DIM),
    )
    return pl.pallas_call(
        hand_over,
        out_shape=(out, out, out),
        in_specs=[vmem] * 3,
        out_specs=(hbm, hbm, hbm),
        scratch_shapes=[dma((3,))],
        name="hand_over",
    )(*(pltpu.with_memory_space_constraint(x, pltpu.VMEM) for x in grads))


def solution(mesh):
    return jax.shard_map(
        body,
        mesh=mesh,
        in_specs=(
            P("ctx", "head"),
            P("ctx", "head"),
            P("ctx", "head"),
            P("head", "ctx"),
            P("ctx", "head"),
            P("head"),
        ),
        out_specs=(P("ctx", "head"), P("ctx", "head"), P("ctx", "head")),
        check_vma=False,
    )
```
